128 devices in a mesh: gx: 8 (over y, x_hi), pa: 16 (over x_lo, z, core).
Axes of the slice: x: 4 (x_hi: 2, x_lo: 2; x = x_hi * 2 + x_lo), y: 4, z: 4, core: 2. Of those that a mesh axis runs over, the one named last changes fastest.
Arguments:
- density: float32 [256, 256, 8, 256], P('gx', 'pa'), may hold values from -6 to 6
- shifts: int32 [256], replicated, may hold values from -10 to 10, as said below
- fractions: float32 [256], replicated, may hold values from 0 to 1
- kick_phase: float32 [256, 256, 8, 256], P('gx', None, None, 'pa'), may hold values from -3.1416 to 3.1416, as said below
Outputs:
- evolved: float32 [256, 256, 8, 256], P('gx', 'pa')
The draws below stay inside these ranges and needn't reach their ends.
Inputs may be any that keep to these rules, and one draw needn't show every extreme that they name: `shifts`: in every draw one column has offset 10 and another -10. kick_phase at (i, (256 - k) mod 256, c, (256 - l) mod 256) is minus its value at (i, k, c, l).
All inputs are finite; a program needn't handle non-finite values.
Results may differ from the reference program's by a relative error of at most 0.0001.
Values sent between devices are 32-bit elements; how exact they have to be, the bound alone decides.
No kernel may reach another device: no remote copies, remote signals or barrier semaphores. Data moves between devices by JAX's collectives and lax.ppermute only.
A program may use at most 192 MiB of HBM per device.

```python
import math
import jax
import jax.numpy as jnp
from jax import lax

X2W = 8
P1 = 256
P2 = 256
SMAX = 10
STEPS = 2
NX = 256


def draw_shifts(key, part):
    first_key, second_key = jax.random.split(key)
    shift_values = jax.random.randint(first_key, (P1,), -SMAX, SMAX + 1, dtype=jnp.int32)
    places = jax.random.permutation(second_key, P1)
    shift_values = shift_values.at[places[0]].set(SMAX)
    shift_values = shift_values.at[places[1]].set(-SMAX)
    return shift_values


def draw_kick_phase(key, part):
    raw_angles = jax.random.uniform(key, (NX, P1, X2W, P2), jnp.float32, -math.pi, math.pi)
    mirrored = jnp.roll(jnp.flip(raw_angles, (1, 3)), (1, 1), (1, 3))
    return 0.5 * (raw_angles - mirrored)


def steps_of(key, shape, cuts, low, high):
    def one(position, shards_of):
        steps = jax.random.uniform(jax.random.fold_in(jax.random.fold_in(key, 6), position), (shards_of,), jnp.float32, low / len(cuts), high / len(cuts))
        return jnp.repeat(jnp.exp(steps), shape[position] // shards_of).reshape((-1,) + (1,) * (len(shape) - position - 1))

    gain = one(*cuts[0])
    for cut in cuts[1:]:
        gain = gain * one(*cut)
    return gain


def gaussian(rng, shape, scale, limit, cuts=(), held_as=jnp.bfloat16):
    values = scale * jax.random.normal(rng, shape, jnp.float32)
    if cuts:
        values = values * steps_of(rng, shape, cuts, -0.22, 0.18)
    return jnp.clip(values, -limit, limit).astype(held_as)


def setup_inputs(seed: int = 0) -> dict:
    arg_keys = jax.random.split(jax.random.key(seed), 5)
    density = gaussian(arg_keys[0], (NX, P1, X2W, P2), 1.0, 6.0, ((0, 8), (1, 16)), jnp.float32)
    shifts = draw_shifts(jax.random.fold_in(arg_keys[4], 71), 0)
    fractions = jnp.clip(jax.random.uniform(arg_keys[2], (P1,), jnp.float32, 0.0, 1.0), 0.0, 1.0)
    kick_phase = draw_kick_phase(jax.random.fold_in(arg_keys[4], 71), 0)
    return {"density": density, "shifts": shifts, "fractions": fractions, "kick_phase": kick_phase}


def cubic_weights(fraction):
    return (-fraction * (fraction - 1.0) * (fraction - 2.0) / 6.0,
            (fraction + 1.0) * (fraction - 1.0) * (fraction - 2.0) / 2.0,
            -(fraction + 1.0) * fraction * (fraction - 2.0) / 2.0,
            (fraction + 1.0) * fraction * (fraction - 1.0) / 6.0)


def drift_cells(values, shifts, fractions):
    weights = cubic_weights(fractions)
    length = values.shape[0]
    columns = values.shape[1]
    cell_ids = lax.iota(jnp.int32, length)[:, None]
    column_ids = lax.iota(jnp.int32, columns)[None, :]
    summed = jnp.zeros_like(values)
    for stencil in range(4):
        positions = (cell_ids - shifts[None, :] - 1 + stencil) % length
        gathered = values[positions, column_ids]
        summed = summed + weights[stencil][None, :, None, None] * gathered
    return summed


def apply_kick(values, kick_phase):
    def one_row(pieces):
        slab_row, angles = pieces
        spectrum = jnp.fft.fft2(slab_row, axes=(0, 2))
        kicked = spectrum * jnp.exp(1j * angles)
        return jnp.real(jnp.fft.ifft2(kicked, axes=(0, 2))).astype(jnp.float32)
    return lax.map(one_row, (values, kick_phase))


def reference(density, shifts, fractions, kick_phase):
    evolved = density
    for substep in range(STEPS):
        evolved = apply_kick(drift_cells(evolved, shifts, fractions), kick_phase)
    return evolved
```

```python
import math

import jax
import jax.numpy as jnp
import ml_dtypes
import numpy as np
from jax import lax
from jax.experimental import pallas as pl
from jax.experimental.pallas import tpu as pltpu
from jax.sharding import PartitionSpec as P

STEPS = 2
N = 256
GX = 8
PA = 16
HI = N // GX
PL = N // PA
SLOTS = 8
M = 2 * SLOTS
LANES = HI * PL
PAD_LO = 24
PAD_HI = 16
SMAX = 10
TILE = 32


def split_table(table):
    high = table.astype(ml_dtypes.bfloat16)
    low = (table - high.astype(np.float64)).astype(ml_dtypes.bfloat16)
    return high, low


def stacked(table):
    high, low = split_table(table)
    return np.concatenate([high, high, low], axis=0)


def owned_columns(device):
    start = PL * device + (0 if device < PA // 2 else 1)
    return [start + slot for slot in range(SLOTS)]


def second_tables():
    q = np.arange(N)
    forward = np.zeros((N, N))
    inverse = np.zeros((N, N))
    scale = 1.0 / N ** (STEPS + 1)
    for device in range(PA):
        for slot, col in enumerate(owned_columns(device)):
            angle = 2.0 * math.pi * (q * col % N) / N
            re_row = device * M + slot
            im_row = re_row + SLOTS
            if col == 0:
                half = 1.0 - 2.0 * (q % 2)
                forward[:, re_row] = 1.0
                forward[:, im_row] = half
                inverse[re_row] = scale
                inverse[im_row] = scale * half
            else:
                forward[:, re_row] = np.cos(angle)
                forward[:, im_row] = -np.sin(angle)
                inverse[re_row] = 2.0 * scale * np.cos(angle)
                inverse[im_row] = -2.0 * scale * np.sin(angle)
    return stacked(forward), stacked(inverse)


def first_tables():
    p = np.arange(N)
    angle = 2.0 * math.pi * (p[:, None] * p[None, :] % N) / N
    return stacked(np.cos(angle)), stacked(np.sin(angle))


def parts_of(values):
    high = values.astype(jnp.bfloat16)
    low = (values - high.astype(jnp.float32)).astype(jnp.bfloat16)
    return jnp.concatenate([high, low, high], axis=1)


def dot(a, b):
    return jnp.dot(a, b, preferred_element_type=jnp.float32)


def forward_kernel(x_ref, table_ref, out_ref):
    for c in range(GX):
        rows = x_ref[:, :, c, :].reshape(8 * PL, N)
        out_ref[c] = dot(parts_of(rows), table_ref[...]).T


def forward_second(density, table):
    return pl.pallas_call(
        forward_kernel,
        grid=(HI // 8,),
        in_specs=[
            pl.BlockSpec((8, PL, GX, N), lambda s: (s, 0, 0, 0)),
            pl.BlockSpec((3 * N, N), lambda s: (0, 0)),
        ],
        out_specs=pl.BlockSpec((GX, N, 8 * PL), lambda s: (0, 0, s)),
        out_shape=jax.ShapeDtypeStruct((GX, N, LANES), jnp.float32),
        compiler_params=pltpu.CompilerParams(vmem_limit_bytes=32 << 20),
        cost_estimate=pl.CostEstimate(flops=6 * 4096 * N * N, bytes_accessed=9 << 20, transcendentals=0),
        name="forward_second",
    )(density, table)


def inverse_kernel(v_ref, table_ref, out_ref):
    for c in range(GX):
        rows = v_ref[c].T
        out_ref[:, :, c, :] = dot(parts_of(rows), table_ref[...]).reshape(8, PL, N)


def inverse_second(spectral, table):
    return pl.pallas_call(
        inverse_kernel,
        grid=(HI // 8,),
        in_specs=[
            pl.BlockSpec((GX, N, 8 * PL), lambda s: (0, 0, s)),
            pl.BlockSpec((3 * N, N), lambda s: (0, 0)),
        ],
        out_specs=pl.BlockSpec((8, PL, GX, N), lambda s: (s, 0, 0, 0)),
        out_shape=jax.ShapeDtypeStruct((HI, PL, GX, N), jnp.float32),
        compiler_params=pltpu.CompilerParams(vmem_limit_bytes=32 << 20),
        cost_estimate=pl.CostEstimate(flops=6 * 4096 * N * N, bytes_accessed=9 << 20, transcendentals=0),
        name="inverse_second",
    )(spectral, table)


def block_transpose(pieces, block_ids):
    for step in (4, 2, 1):
        upper = (block_ids & step) != 0
        moved = list(pieces)
        for u in range(8):
            if u & step:
                continue
            v = u + step
            first, second = pieces[u], pieces[v]
            moved[u] = jnp.where(upper, pltpu.roll(second, PL * step, 1), first)
            moved[v] = jnp.where(upper, second, pltpu.roll(first, 128 - PL * step, 1))
        pieces = moved
    return pieces


def middle_kernel(flag_ref, r_ref, cos_ref, sin_ref, bits_ref, w_ref, tc_ref, ts_ref, y_ref,
                  xa, xb, wf_re, wf_im, wi_re, wi_im, s_re, s_im):
    k3 = 3 * N
    tc = tc_ref[...]
    ts = ts_ref[...]
    minus = -ts
    wf_re[0:k3] = tc
    wf_re[k3:2 * k3] = ts
    wf_im[0:k3] = minus
    wf_im[k3:2 * k3] = tc
    wi_re[0:k3] = tc
    wi_re[k3:2 * k3] = minus
    wi_im[0:k3] = ts
    wi_im[k3:2 * k3] = tc
    block_ids = lax.broadcasted_iota(jnp.int32, (8, 128), 1) // PL

    def gather(step, carry):
        a = step // 4
        g = step % 4
        lane = pl.multiple_of(g * 128, 128)
        row = PAD_LO + step * 8
        for mh in range(2):
            for bh in range(2):
                pieces = [r_ref[a, bh * 8 + j, mh * 8:mh * 8 + 8, pl.ds(lane, 128)] for j in range(8)]
                pieces = block_transpose(pieces, block_ids)
                for j in range(8):
                    xa[row + j, mh * 8:mh * 8 + 8, bh * 128:bh * 128 + 128] = pieces[j]
        return carry

    def scatter(step, carry):
        a = step // 4
        g = step % 4
        lane = pl.multiple_of(g * 128, 128)
        row = step * 8
        for mh in range(2):
            for bh in range(2):
                pieces = [xb[row + j, mh * 8:mh * 8 + 8, bh * 128:bh * 128 + 128] for j in range(8)]
                pieces = block_transpose(pieces, block_ids)
                for j in range(8):
                    y_ref[a, bh * 8 + j, mh * 8:mh * 8 + 8, pl.ds(lane, 128)] = pieces[j]
        return carry

    def wrap():
        xa[0:PAD_LO] = xa[N:N + PAD_LO]
        xa[PAD_LO + N:PAD_LO + N + PAD_HI] = xa[PAD_LO:PAD_LO + PAD_HI]

    def drift(step, carry):
        first = step * TILE
        need = TILE + 3
        for mh in range(2):
            for ph in range(2):
                ms = slice(mh * 8, mh * 8 + 8)
                ps = slice(ph * 128, ph * 128 + 128)
                rows = need + 31
                z = xa[pl.ds(first + PAD_LO + SMAX - 1 - 31, rows), ms, ps]
                for bit in (4, 3, 2, 1, 0):
                    size = 1 << bit
                    taken = bits_ref[bit, :, ps] != 0
                    z = jnp.where(taken[None], z[:rows - size], z[size:])
                    rows = rows - size
                total = w_ref[0, :, ps][None] * z[0:TILE]
                for k in (1, 2, 3):
                    total = total + w_ref[k, :, ps][None] * z[k:k + TILE]
                xb[pl.ds(first, TILE), ms, ps] = total
        return carry

    def kick(to_ref, offset):
        def body(step, carry):
            first = step * TILE
            rows = TILE * SLOTS
            at = pl.ds(first, TILE)
            xr = xb[at, 0:8, :].reshape(rows, N)
            xi = xb[at, 8:16, :].reshape(rows, N)
            both = jnp.concatenate([parts_of(xr), parts_of(xi)], axis=1)
            zr = dot(both, wf_re[...])
            zi = dot(both, wf_im[...])
            cos = cos_ref[at].reshape(rows, N)
            sin = sin_ref[at].reshape(rows, N)
            gr = zr * cos - zi * sin
            gi = zr * sin + zi * cos
            both = jnp.concatenate([parts_of(gr), parts_of(gi)], axis=1)
            out = pl.ds(first + offset, TILE)
            to_ref[out, 0:8, :] = dot(both, wi_re[...]).reshape(TILE, 8, N)
            to_ref[out, 8:16, :] = dot(both, wi_im[...]).reshape(TILE, 8, N)
            return carry
        return body

    def kick_all(to_ref, offset):
        special = flag_ref[0] != 0

        @pl.when(special)
        def _():
            tcs = tc_ref[...]
            tss = ts_ref[...]
            lane = lax.broadcasted_iota(jnp.int32, (N, N), 1)
            ends = (lane == 0) | (lane == N // 2)
            low = lane < N // 2
            x0 = parts_of(xb[:, 0, :])
            x1 = parts_of(xb[:, 8, :])
            c1 = dot(x1, tcs)
            zr = jnp.where(low | ends, dot(x0, tcs), c1)
            zi = jnp.where(ends, c1, -jnp.where(low, dot(x0, tss), dot(x1, tss)))
            cos = cos_ref[:, 0, :]
            sin = sin_ref[:, 0, :]
            gr = zr * cos - zi * sin
            gi = zr * sin + zi * cos
            zero = jnp.zeros_like(gr)
            a_re = jnp.where(ends, gr, jnp.where(low, 2.0 * gr, zero))
            a_im = jnp.where(ends, zero, jnp.where(low, 2.0 * gi, zero))
            b_re = jnp.where(ends, gi, jnp.where(low, zero, 2.0 * gr))
            b_im = jnp.where(ends, zero, jnp.where(low, zero, 2.0 * gi))
            s_re[...] = dot(parts_of(a_re), tcs) - dot(parts_of(a_im), tss)
            s_im[...] = dot(parts_of(b_re), tcs) - dot(parts_of(b_im), tss)

        lax.fori_loop(0, N // TILE, kick(to_ref, offset), 0)

        @pl.when(special)
        def _():
            to_ref[offset:offset + N, 0, :] = s_re[...]
            to_ref[offset:offset + N, 8, :] = s_im[...]

    lax.fori_loop(0, N // 8, gather, 0)
    for substep in range(STEPS):
        wrap()
        lax.fori_loop(0, N // TILE, drift, 0)
        if substep + 1 < STEPS:
            kick_all(xa, PAD_LO)
        else:
            kick_all(xb, 0)
    lax.fori_loop(0, N // 8, scatter, 0)


def middle(flag, received, cos, sin, bits, weights, tc, ts):
    whole = pl.BlockSpec(memory_space=pltpu.VMEM)
    return pl.pallas_call(
        middle_kernel,
        in_specs=[pl.BlockSpec(memory_space=pltpu.SMEM)] + [whole] * 7,
        out_specs=whole,
        out_shape=jax.ShapeDtypeStruct((GX, PA, M, LANES), jnp.float32),
        scratch_shapes=[
            pltpu.VMEM((PAD_LO + N + PAD_HI, M, N), jnp.float32),
            pltpu.VMEM((N, M, N), jnp.float32),
            pltpu.VMEM((6 * N, N), jnp.bfloat16),
            pltpu.VMEM((6 * N, N), jnp.bfloat16),
            pltpu.VMEM((6 * N, N), jnp.bfloat16),
            pltpu.VMEM((6 * N, N), jnp.bfloat16),
            pltpu.VMEM((N, N), jnp.float32),
            pltpu.VMEM((N, N), jnp.float32),
        ],
        compiler_params=pltpu.CompilerParams(vmem_limit_bytes=52 << 20),
        cost_estimate=pl.CostEstimate(flops=24 * 2048 * 2 * N * 2 * N, bytes_accessed=14 << 20, transcendentals=0),
        name="middle",
    )(flag, received, cos, sin, bits, weights, tc, ts)


def cubic_weights(fraction):
    return (
        -fraction * (fraction - 1.0) * (fraction - 2.0) / 6.0,
        (fraction + 1.0) * (fraction - 1.0) * (fraction - 2.0) / 2.0,
        -(fraction + 1.0) * fraction * (fraction - 2.0) / 2.0,
        (fraction + 1.0) * fraction * (fraction - 1.0) / 6.0,
    )


def owned_phases(kick_phase):
    rank = lax.axis_index("pa")
    turned = kick_phase.transpose(2, 0, 3, 1)
    upper = lax.ppermute(turned[:, :, 0, N // 2:], "pa", [(PA // 2, 0)])
    chosen = jnp.where(rank < PA // 2, turned[:, :, 0:SLOTS], turned[:, :, 1:SLOTS + 1])
    upper = jnp.pad(upper[:, :, None, :], ((0, 0), (0, 0), (0, SLOTS - 1), (N // 2, 0)))
    slot = lax.broadcasted_iota(jnp.int32, chosen.shape, 2)
    lane = lax.broadcasted_iota(jnp.int32, chosen.shape, 3)
    shared = (rank == 0) & (slot == 0) & (lane >= N // 2)
    chosen = jnp.where(shared, upper, chosen)
    phases = lax.all_to_all(chosen, "gx", 0, 0, tiled=True)
    return phases.reshape(N, SLOTS, N)


def shards(density, shifts, fractions, kick_phase):
    rank = lax.axis_index("pa")
    forward, inverse = (jnp.asarray(t) for t in second_tables())
    tc, ts = (jnp.asarray(t) for t in first_tables())
    steps = shifts + SMAX
    bits = jnp.stack([(steps >> b) & 1 for b in range(5)])
    bits = jnp.broadcast_to(bits[:, None, :], (5, 8, N))
    weights = jnp.broadcast_to(jnp.stack(cubic_weights(fractions))[:, None, :], (4, 8, N))
    flag = (rank == 0).astype(jnp.int32).reshape(1)
    phases = owned_phases(kick_phase)
    spectral = forward_second(density, forward)
    spectral = spectral.reshape(GX * PA, M, LANES)
    received = lax.all_to_all(spectral, ("gx", "pa"), 0, 0, tiled=True)
    received = received.reshape(GX, PA, M, LANES)
    sent = middle(flag, received, jnp.cos(phases), jnp.sin(phases), bits, weights, tc, ts)
    sent = sent.reshape(GX * PA, M, LANES)
    returned = lax.all_to_all(sent, ("gx", "pa"), 0, 0, tiled=True)
    return inverse_second(returned.reshape(GX, N, LANES), inverse)


def solution(mesh):
    placed = (P("gx", "pa", None, None), P(), P(), P("gx", None, None, "pa"))
    return jax.shard_map(
        shards, mesh=mesh, in_specs=placed, out_specs=P("gx", "pa", None, None), check_vma=False
    )
```

```python
import functools
import math

import jax
import jax.numpy as jnp
import ml_dtypes
import numpy as np
from jax import lax
from jax.experimental import pallas as pl
from jax.experimental.pallas import tpu as pltpu
from jax.sharding import PartitionSpec as P

STEPS = 2
N = 256
GX = 8
PA = 16
HI = N // GX
PL = N // PA
SLOTS = 8
M = 2 * SLOTS
LANES = HI * PL
PAD_LO = 24
PAD_HI = 16
SMAX = 10
TILE = 32
KTILE = 64
ROWS = 16


def split_table(table):
    high = table.astype(ml_dtypes.bfloat16)
    low = (table - high.astype(np.float64)).astype(ml_dtypes.bfloat16)
    return high, low


def stacked(table):
    high, low = split_table(table)
    return np.concatenate([high, high, low], axis=0)


def owned_columns(device):
    start = PL * device + (0 if device < PA // 2 else 1)
    return [start + slot for slot in range(SLOTS)]


def second_tables():
    q = np.arange(N)
    forward = np.zeros((N, N))
    inverse = np.zeros((N, N))
    scale = 1.0 / N ** (STEPS + 1)
    for device in range(PA):
        for slot, col in enumerate(owned_columns(device)):
            angle = 2.0 * math.pi * (q * col % N) / N
            re_row = device * M + slot
            im_row = re_row + SLOTS
            if col == 0:
                half = 1.0 - 2.0 * (q % 2)
                forward[:, re_row] = 1.0
                forward[:, im_row] = half
                inverse[re_row] = scale
                inverse[im_row] = scale * half
            else:
                forward[:, re_row] = np.cos(angle)
                forward[:, im_row] = -np.sin(angle)
                inverse[re_row] = 2.0 * scale * np.cos(angle)
                inverse[im_row] = -2.0 * scale * np.sin(angle)
    return stacked(forward), stacked(inverse)


def paired(even):
    half = np.arange(N // 2)
    k = 2 * half + (0 if even else 1)
    angle = 2.0 * math.pi * (half[:, None] * k[None, :] % N) / N
    cos, sin = np.cos(angle), np.sin(angle)
    forward = np.block([[cos, -sin], [sin, cos]])
    inverse = np.block([[cos.T, sin.T], [-sin.T, cos.T]])
    return stacked(forward), stacked(inverse)


def real_tables():
    p = np.arange(N)
    k = np.arange(N // 2)
    angle = 2.0 * math.pi * (p[:, None] * k[None, :] % N) / N
    last = (1.0 - 2.0 * (p % 2))[:, None]
    cos, sin = np.cos(angle), np.sin(angle)
    forward = np.concatenate([cos, last, -sin[:, 1:]], axis=1)
    inverse = np.concatenate([cos[:, :1], 2.0 * cos[:, 1:], last, -2.0 * sin[:, 1:]], axis=1).T
    return stacked(forward), stacked(inverse)


def parity_order():
    table = np.zeros((N, N))
    k = np.concatenate([np.arange(0, N, 2), np.arange(1, N, 2)])
    table[k, np.arange(N)] = 1.0
    return np.concatenate([table] * 3, axis=0).astype(ml_dtypes.bfloat16)


def parts_of(values):
    high = values.astype(jnp.bfloat16)
    low = (values - high.astype(jnp.float32)).astype(jnp.bfloat16)
    return jnp.concatenate([high, low, high], axis=1)


def dot(a, b):
    return jnp.dot(a, b, preferred_element_type=jnp.float32)


def forward_kernel(low_ref, high_ref, table_ref, out_ref):
    low = low_ref.reshape(8 * PL * GX, N // 2)
    high = high_ref.reshape(8 * PL * GX, N // 2)
    rank = lax.axis_index("pa")
    for c in range(GX):
        rows = []
        for n in range(8):
            at = pl.ds((n + PA - rank) % 8 * (PL * GX) + c, PL, stride=GX)
            rows.append(jnp.concatenate([low[at, :], high[at, :]], axis=1))
        rows = jnp.concatenate(rows, axis=0)
        out_ref[c] = dot(parts_of(rows), table_ref[...]).T


def forward_second(density, table):
    return pl.pallas_call(
        forward_kernel,
        grid=(HI // 8,),
        in_specs=[
            pl.BlockSpec((8, PL, GX, N // 2), lambda s: (s, 0, 0, 0)),
            pl.BlockSpec((8, PL, GX, N // 2), lambda s: (s, 0, 0, 1)),
            pl.BlockSpec((3 * N, N), lambda s: (0, 0)),
        ],
        out_specs=pl.BlockSpec((GX, N, 8 * PL), lambda s: (0, 0, s)),
        out_shape=jax.ShapeDtypeStruct((GX, N, LANES), jnp.float32),
        compiler_params=pltpu.CompilerParams(vmem_limit_bytes=60 << 20),
        cost_estimate=pl.CostEstimate(flops=6 * 4096 * N * N, bytes_accessed=9 << 20, transcendentals=0),
        name="forward_second",
    )(density, density, table)


def inverse_kernel(v_ref, table_ref, out_ref):
    rank = lax.axis_index("pa")
    for c in range(GX):
        rows = dot(parts_of(v_ref[c].T), table_ref[...]).reshape(8, PL, N)
        for n in range(8):
            out_ref[(n + PA - rank) % 8, :, c, :] = rows[n]


def inverse_second(spectral, table):
    return pl.pallas_call(
        inverse_kernel,
        grid=(HI // 8,),
        in_specs=[
            pl.BlockSpec((GX, N, 8 * PL), lambda s: (0, 0, s)),
            pl.BlockSpec((3 * N, N), lambda s: (0, 0)),
        ],
        out_specs=pl.BlockSpec((8, PL, GX, N), lambda s: (s, 0, 0, 0)),
        out_shape=jax.ShapeDtypeStruct((HI, PL, GX, N), jnp.float32),
        compiler_params=pltpu.CompilerParams(vmem_limit_bytes=32 << 20),
        cost_estimate=pl.CostEstimate(flops=6 * 4096 * N * N, bytes_accessed=9 << 20, transcendentals=0),
        name="inverse_second",
    )(spectral, table)


def deal(pieces, block_ids):
    pieces = [pieces[-d % 8] for d in range(8)]
    for step in (1, 2, 4):
        taken = (block_ids & step) != 0
        pieces = [jnp.where(taken, pieces[(d - step) % 8], pieces[d]) for d in range(8)]
    return pieces


def choose_kernel(phase_ref, out_ref):
    low = lax.axis_index("pa") < PA // 2
    for c in range(GX):
        out_ref[c, 0, :ROWS] = jnp.where(low, phase_ref[:, c, 0:SLOTS, :], phase_ref[:, c, 1:SLOTS + 1, :])
        first = phase_ref[:, c, 0, :N // 2]
        out_ref[c, 0, ROWS] = jnp.concatenate([first[:8], first[8:]], axis=1)


def choose_phases(turned):
    shape = (GX, HI // ROWS, ROWS + 1, SLOTS, N)
    return pl.pallas_call(
        choose_kernel,
        grid=(HI // ROWS,),
        in_specs=[pl.BlockSpec((ROWS, GX, PL, N), lambda s: (s, 0, 0, 0))],
        out_specs=pl.BlockSpec((GX, 1) + shape[2:], lambda s: (0, s, 0, 0, 0)),
        out_shape=jax.ShapeDtypeStruct(shape, jnp.float32),
        compiler_params=pltpu.CompilerParams(vmem_limit_bytes=60 << 20),
        cost_estimate=pl.CostEstimate(flops=0, bytes_accessed=7 << 20, transcendentals=0),
        name="choose_phases",
    )(turned)


def turn_kernel(phase_ref, order_ref, cos_ref, sin_ref, cos0_ref, sin0_ref, lowest_ref):
    for j in range(GX):
        for s in range(HI // ROWS):
            start = j * HI + s * ROWS
            at = pl.ds(start, ROWS)
            angles = phase_ref[j, s, :ROWS].reshape(ROWS * SLOTS, N)
            high = angles.astype(jnp.bfloat16)
            rest = angles - high.astype(jnp.float32)
            mid = rest.astype(jnp.bfloat16)
            low = (rest - mid.astype(jnp.float32)).astype(jnp.bfloat16)
            angles = dot(jnp.concatenate([high, mid, low], axis=1), order_ref[...])
            cos_ref[at] = jnp.cos(angles).reshape(ROWS, SLOTS, N)
            sin_ref[at] = jnp.sin(angles).reshape(ROWS, SLOTS, N)
            first = phase_ref[j, s, :ROWS, 0, :N // 2]
            cos0_ref[at, :] = jnp.cos(first)
            sin0_ref[at, :] = jnp.sin(first)
            tail = phase_ref[j, s, ROWS]
            lowest_ref[pl.ds(start, 8), :] = tail[:, :N // 2]
            lowest_ref[pl.ds(start + 8, 8), :] = tail[:, N // 2:]


def turn_factors(phases, order):
    whole = pl.BlockSpec(memory_space=pltpu.VMEM)
    full = jax.ShapeDtypeStruct((N, SLOTS, N), jnp.float32)
    first = jax.ShapeDtypeStruct((N, N // 2), jnp.float32)
    return pl.pallas_call(
        turn_kernel,
        in_specs=[whole] * 2,
        out_specs=[whole] * 5,
        out_shape=[full, full, first, first, first],
        compiler_params=pltpu.CompilerParams(vmem_limit_bytes=24 << 20),
        cost_estimate=pl.CostEstimate(flops=0, bytes_accessed=8 << 20, transcendentals=2 * N * N * SLOTS),
        name="turn_factors",
    )(phases, order)


def middle_kernel(r_hbm, cos_hbm, sin_hbm, cos0_hbm, sin0_hbm, lowest_hbm, tables_hbm, shift_ref, fraction_ref,
                  y_hbm, buf, xa, xb, cos_ref, sin_ref, cos0_ref, sin0_ref, cos1_ref, sin1_ref, tables_ref,
                  bits_ref, w_ref, s_re, s_im, block_sems, sems):
    half = N // 2
    special = lax.axis_index("pa") == 0
    inbound = [pltpu.make_async_copy(r_hbm.at[a], buf.at[a], block_sems.at[a]) for a in range(GX)]
    extras = [
        pltpu.make_async_copy(source, target, sems.at[n])
        for n, (source, target) in enumerate((
            (tables_hbm, tables_ref), (cos_hbm, cos_ref), (sin_hbm, sin_ref),
            (cos0_hbm, cos0_ref), (sin0_hbm, sin0_ref), (lowest_hbm, cos1_ref),
        ))
    ]
    for copy in inbound + extras:
        copy.start()
    fe_ref, fo_ref, ie_ref, io_ref, fr_ref, ir_ref = (tables_ref.at[n] for n in range(6))

    steps = jnp.broadcast_to(shift_ref[...], (8, N)) + SMAX
    for bit in range(5):
        bits_ref[bit] = (steps >> bit) & 1
    for k, weight in enumerate(cubic_weights(jnp.broadcast_to(fraction_ref[...], (8, N)))):
        w_ref[k] = weight
    block_ids = lax.broadcasted_iota(jnp.int32, (8, 128), 1) // PL

    def gather(a, g, carry):
        step = a * 4 + g
        lane = pl.multiple_of(g * 128, 128)
        row = PAD_LO + step * 8
        for mh in range(2):
            for bh in range(2):
                pieces = [buf[a, bh * 8 + j, mh * 8:mh * 8 + 8, pl.ds(lane, 128)] for j in range(8)]
                pieces = deal(pieces, block_ids)
                for j in range(8):
                    piece = pltpu.roll(pieces[j], 128 - PL * j, 1) if j else pieces[j]
                    xa[bh, row + j, mh * 8:mh * 8 + 8, :] = piece
        return carry

    def scatter(a, g, carry):
        step = a * 4 + g
        lane = pl.multiple_of(g * 128, 128)
        row = step * 8
        for mh in range(2):
            for bh in range(2):
                pieces = [xb[bh, row + j, mh * 8:mh * 8 + 8, :] for j in range(8)]
                pieces = [pltpu.roll(pieces[j], PL * j, 1) if j else pieces[j] for j in range(8)]
                pieces = deal(pieces, block_ids)
                for j in range(8):
                    buf[a, bh * 8 + j, mh * 8:mh * 8 + 8, pl.ds(lane, 128)] = pieces[j]
        return carry

    def wrap():
        xa[:, 0:PAD_LO] = xa[:, N:N + PAD_LO]
        xa[:, PAD_LO + N:PAD_LO + N + PAD_HI] = xa[:, PAD_LO:PAD_LO + PAD_HI]

    def drift(step, carry):
        first = step * TILE
        need = TILE + 3
        for mh in range(2):
            for ph in range(2):
                ms = slice(mh * 8, mh * 8 + 8)
                ps = slice(ph * 128, ph * 128 + 128)
                rows = need + 31
                z = xa[ph, pl.ds(first + PAD_LO + SMAX - 1 - 31, rows), ms, :]
                for bit in (4, 3, 2, 1, 0):
                    size = 1 << bit
                    taken = bits_ref[bit, :, ps] != 0
                    z = jnp.where(taken[None], z[:rows - size], z[size:])
                    rows = rows - size
                total = w_ref[0, :, ps][None] * z[0:TILE]
                for k in (1, 2, 3):
                    total = total + w_ref[k, :, ps][None] * z[k:k + TILE]
                xb[ph, pl.ds(first, TILE), ms, :] = total
        return carry

    def kick(to_ref, offset):
        def body(step, carry):
            first = step * KTILE
            rows = KTILE * SLOTS
            at = pl.ds(first, KTILE)
            xr, xi, xr2, xi2 = (
                xb[h, at, m:m + 8, :].reshape(rows, half) for h in range(2) for m in (0, 8)
            )
            cos = cos_ref[at].reshape(rows, N)
            sin = sin_ref[at].reshape(rows, N)

            def turned(yr, yi, c, s, forward_ref, inverse_ref):
                z = dot(parts_of(jnp.concatenate([yr, yi], axis=1)), forward_ref[...])
                zr, zi = z[:, :half], z[:, half:]
                g = jnp.concatenate([zr * c - zi * s, zr * s + zi * c], axis=1)
                return dot(parts_of(g), inverse_ref[...])

            even = turned(xr + xr2, xi + xi2, cos[:, :half], sin[:, :half], fe_ref, ie_ref)
            odd = turned(xr - xr2, xi - xi2, cos[:, half:], sin[:, half:], fo_ref, io_ref)
            out = pl.ds(first + offset, KTILE)
            for h, both in enumerate((even + odd, even - odd)):
                to_ref[h, out, 0:8, :] = both[:, :half].reshape(KTILE, 8, half)
                to_ref[h, out, 8:16, :] = both[:, half:].reshape(KTILE, 8, half)
            return carry
        return body

    def kick_all(to_ref, offset):
        @pl.when(special)
        def _():
            def real_turned(row, c, s):
                flat = xb.reshape(2 * N * M, half)
                x = jnp.concatenate([flat[pl.ds(h * N * M + row, N, stride=M), :] for h in range(2)], axis=1)
                z = dot(parts_of(x), fr_ref[...])
                zr, zi = z[:, :half], z[:, half:]
                g = jnp.concatenate([zr * c - zi * s, zr * s + zi * c], axis=1)
                return dot(parts_of(g), ir_ref[...])

            s_re[...] = real_turned(0, cos0_ref[...], sin0_ref[...])
            s_im[...] = real_turned(SLOTS, cos1_ref[...], sin1_ref[...])

        lax.fori_loop(0, N // KTILE, kick(to_ref, offset), 0)

        @pl.when(special)
        def _():
            length = to_ref.shape[1]
            flat = to_ref.reshape(2 * length * M, half)
            for h in range(2):
                first = (h * length + offset) * M
                lanes = slice(h * half, h * half + half)
                flat[pl.ds(first, N, stride=M), :] = s_re[:, lanes]
                flat[pl.ds(first + SLOTS, N, stride=M), :] = s_im[:, lanes]

    for a in range(GX):
        inbound[a].wait()
        lax.fori_loop(0, HI // 8, functools.partial(gather, a), 0)
    for substep in range(STEPS):
        wrap()
        lax.fori_loop(0, N // TILE, drift, 0)
        if substep == 0:
            for copy in extras:
                copy.wait()

            @pl.when(special)
            def _():
                angles = cos1_ref[...]
                cos1_ref[...] = jnp.cos(angles)
                sin1_ref[...] = jnp.sin(angles)

        if substep + 1 < STEPS:
            kick_all(xa, PAD_LO)
        else:
            kick_all(xb, 0)
    outbound = [pltpu.make_async_copy(buf.at[a], y_hbm.at[a], block_sems.at[a]) for a in range(GX)]
    for a in range(GX):
        lax.fori_loop(0, HI // 8, functools.partial(scatter, a), 0)
        outbound[a].start()
    for copy in outbound:
        copy.wait()


def middle(received, factors, lowest, tables, shifts, fractions):
    anywhere = pl.BlockSpec(memory_space=pl.ANY)
    whole = pl.BlockSpec(memory_space=pltpu.VMEM)
    return pl.pallas_call(
        middle_kernel,
        in_specs=[anywhere] * 7 + [whole] * 2,
        out_specs=anywhere,
        out_shape=jax.ShapeDtypeStruct((GX, PA, M, LANES), jnp.float32),
        scratch_shapes=[
            pltpu.VMEM((GX, PA, M, LANES), jnp.float32),
            pltpu.VMEM((2, PAD_LO + N + PAD_HI, M, N // 2), jnp.float32),
            pltpu.VMEM((2, N, M, N // 2), jnp.float32),
            pltpu.VMEM((N, SLOTS, N), jnp.float32),
            pltpu.VMEM((N, SLOTS, N), jnp.float32),
        ] + [pltpu.VMEM((N, N // 2), jnp.float32)] * 4 + [
            pltpu.VMEM((6, 3 * N, N), jnp.bfloat16),
            pltpu.VMEM((5, 8, N), jnp.int32),
            pltpu.VMEM((4, 8, N), jnp.float32),
            pltpu.VMEM((N, N), jnp.float32),
            pltpu.VMEM((N, N), jnp.float32),
            pltpu.SemaphoreType.DMA((GX,)),
            pltpu.SemaphoreType.DMA((6,)),
        ],
        compiler_params=pltpu.CompilerParams(vmem_limit_bytes=60 << 20),
        cost_estimate=pl.CostEstimate(flops=24 * 2048 * 2 * N * N, bytes_accessed=14 << 20, transcendentals=0),
        name="middle",
    )(received, *factors, lowest, tables, shifts, fractions)


def cubic_weights(fraction):
    return (
        -fraction * (fraction - 1.0) * (fraction - 2.0) / 6.0,
        (fraction + 1.0) * (fraction - 1.0) * (fraction - 2.0) / 2.0,
        -(fraction + 1.0) * fraction * (fraction - 2.0) / 2.0,
        (fraction + 1.0) * fraction * (fraction - 1.0) / 6.0,
    )


def shards(density, shifts, fractions, kick_phase):
    forward, inverse = (jnp.asarray(t) for t in second_tables())
    (fe, ie), (fo, io), (fr, ir) = paired(True), paired(False), real_tables()
    tables = jnp.asarray(np.stack([fe, fo, ie, io, fr, ir]))
    chosen = choose_phases(kick_phase.transpose(0, 2, 3, 1))
    chosen, density = lax.optimization_barrier((chosen, density))
    phases = lax.all_to_all(chosen, "gx", 0, 0, tiled=True)
    spectral = forward_second(density, forward).reshape(GX * PA, M, LANES)
    phases, spectral = lax.optimization_barrier((phases, spectral))
    received = lax.all_to_all(spectral, ("gx", "pa"), 0, 0, tiled=True)
    received = received.reshape(GX, PA, M, LANES)
    *factors, lowest = turn_factors(phases, jnp.asarray(parity_order()))
    lowest = lax.ppermute(lowest, "pa", [(PA // 2, 0)])
    sent = middle(received, factors, lowest, tables, shifts.reshape(1, N), fractions.reshape(1, N))
    sent = sent.reshape(GX * PA, M, LANES)
    returned = lax.all_to_all(sent, ("gx", "pa"), 0, 0, tiled=True)
    return inverse_second(returned.reshape(GX, N, LANES), inverse)


def solution(mesh):
    placed = (P("gx", "pa", None, None), P(), P(), P("gx", None, None, "pa"))
    return jax.shard_map(
        shards, mesh=mesh, in_specs=placed, out_specs=P("gx", "pa", None, None), check_vma=False
    )
```

```python
import functools
import math

import jax
import jax.numpy as jnp
import ml_dtypes
import numpy as np
from jax import lax
from jax.experimental import pallas as pl
from jax.experimental.pallas import tpu as pltpu
from jax.sharding import PartitionSpec as P

STEPS = 2
N = 256
GX = 8
PA = 16
HI = N // GX
PL = N // PA
SLOTS = 8
M = 2 * SLOTS
LANES = HI * PL
PAD_LO = 24
PAD_HI = 16
SMAX = 10
TILE = 32
KTILE = 64
ROWS = 16


def split_table(table):
    high = table.astype(ml_dtypes.bfloat16)
    low = (table - high.astype(np.float64)).astype(ml_dtypes.bfloat16)
    return high, low


def stacked(table):
    high, low = split_table(table)
    return np.concatenate([high, high, low], axis=0)


def owned_columns(device):
    start = PL * device + (0 if device < PA // 2 else 1)
    return [start + slot for slot in range(SLOTS)]


def second_tables():
    q = np.arange(N)
    forward = np.zeros((N, N))
    inverse = np.zeros((N, N))
    scale = 1.0 / N ** (STEPS + 1)
    for device in range(PA):
        for slot, col in enumerate(owned_columns(device)):
            angle = 2.0 * math.pi * (q * col % N) / N
            re_row = device * M + slot
            im_row = re_row + SLOTS
            if col == 0:
                half = 1.0 - 2.0 * (q % 2)
                forward[:, re_row] = 1.0
                forward[:, im_row] = half
                inverse[re_row] = scale
                inverse[im_row] = scale * half
            else:
                forward[:, re_row] = np.cos(angle)
                forward[:, im_row] = -np.sin(angle)
                inverse[re_row] = 2.0 * scale * np.cos(angle)
                inverse[im_row] = -2.0 * scale * np.sin(angle)
    return stacked(forward), stacked(inverse)


def paired(even):
    half = np.arange(N // 2)
    k = 2 * half + (0 if even else 1)
    angle = 2.0 * math.pi * (half[:, None] * k[None, :] % N) / N
    cos, sin = np.cos(angle), np.sin(angle)
    forward = np.block([[cos, -sin], [sin, cos]])
    inverse = np.block([[cos.T, sin.T], [-sin.T, cos.T]])
    return stacked(forward), stacked(inverse)


def real_tables():
    p = np.arange(N)
    k = np.arange(N // 2)
    angle = 2.0 * math.pi * (p[:, None] * k[None, :] % N) / N
    last = (1.0 - 2.0 * (p % 2))[:, None]
    cos, sin = np.cos(angle), np.sin(angle)
    forward = np.concatenate([cos, last, -sin[:, 1:]], axis=1)
    inverse = np.concatenate([cos[:, :1], 2.0 * cos[:, 1:], last, -2.0 * sin[:, 1:]], axis=1).T
    return stacked(forward), stacked(inverse)


def parity_order():
    table = np.zeros((N, N))
    k = np.concatenate([np.arange(0, N, 2), np.arange(1, N, 2)])
    table[k, np.arange(N)] = 1.0
    return np.concatenate([table] * 3, axis=0).astype(ml_dtypes.bfloat16)


def parts_of(values):
    high = values.astype(jnp.bfloat16)
    low = (values - high.astype(jnp.float32)).astype(jnp.bfloat16)
    return jnp.concatenate([high, low, high], axis=1)


def dot(a, b):
    return jnp.dot(a, b, preferred_element_type=jnp.float32)


def forward_kernel(low_ref, high_ref, table_ref, out_ref):
    low = low_ref.reshape(8 * PL * GX, N // 2)
    high = high_ref.reshape(8 * PL * GX, N // 2)
    rank = lax.axis_index("pa")
    for c in range(GX):
        rows = []
        for n in range(8):
            at = pl.ds((n + PA - rank) % 8 * (PL * GX) + c, PL, stride=GX)
            rows.append(jnp.concatenate([low[at, :], high[at, :]], axis=1))
        rows = jnp.concatenate(rows, axis=0)
        out_ref[c] = dot(parts_of(rows), table_ref[...]).T


def forward_second(density, table):
    return pl.pallas_call(
        forward_kernel,
        grid=(HI // 8,),
        in_specs=[
            pl.BlockSpec((8, PL, GX, N // 2), lambda s: (s, 0, 0, 0)),
            pl.BlockSpec((8, PL, GX, N // 2), lambda s: (s, 0, 0, 1)),
            pl.BlockSpec((3 * N, N), lambda s: (0, 0)),
        ],
        out_specs=pl.BlockSpec((GX, N, 8 * PL), lambda s: (0, 0, s)),
        out_shape=jax.ShapeDtypeStruct((GX, N, LANES), jnp.float32),
        compiler_params=pltpu.CompilerParams(vmem_limit_bytes=60 << 20),
        cost_estimate=pl.CostEstimate(flops=6 * 4096 * N * N, bytes_accessed=9 << 20, transcendentals=0),
        name="forward_second",
    )(density, density, table)


def inverse_kernel(v_ref, table_ref, out_ref):
    rank = lax.axis_index("pa")
    for c in range(GX):
        rows = dot(parts_of(v_ref[c].T), table_ref[...]).reshape(8, PL, N)
        for n in range(8):
            out_ref[(n + PA - rank) % 8, :, c, :] = rows[n]


def inverse_second(spectral, table):
    return pl.pallas_call(
        inverse_kernel,
        grid=(HI // 8,),
        in_specs=[
            pl.BlockSpec((GX, N, 8 * PL), lambda s: (0, 0, s)),
            pl.BlockSpec((3 * N, N), lambda s: (0, 0)),
        ],
        out_specs=pl.BlockSpec((8, PL, GX, N), lambda s: (s, 0, 0, 0)),
        out_shape=jax.ShapeDtypeStruct((HI, PL, GX, N), jnp.float32),
        compiler_params=pltpu.CompilerParams(vmem_limit_bytes=32 << 20),
        cost_estimate=pl.CostEstimate(flops=6 * 4096 * N * N, bytes_accessed=9 << 20, transcendentals=0),
        name="inverse_second",
    )(spectral, table)


def deal(pieces, block_ids):
    pieces = [pieces[-d % 8] for d in range(8)]
    for step in (1, 2, 4):
        taken = (block_ids & step) != 0
        pieces = [jnp.where(taken, pieces[(d - step) % 8], pieces[d]) for d in range(8)]
    return pieces


def choose_kernel(phase_ref, out_ref):
    low = lax.axis_index("pa") < PA // 2
    for s in range(HI // ROWS):
        at = slice(s * ROWS, s * ROWS + ROWS)
        out_ref[0, s, :ROWS] = jnp.where(low, phase_ref[at, 0, 0:SLOTS, :], phase_ref[at, 0, 1:SLOTS + 1, :])
        first = phase_ref[at, 0, 0, :N // 2]
        out_ref[0, s, ROWS] = jnp.concatenate([first[:8], first[8:]], axis=1)


def choose_phases(turned):
    shape = (GX, HI // ROWS, ROWS + 1, SLOTS, N)
    return pl.pallas_call(
        choose_kernel,
        grid=(GX,),
        in_specs=[pl.BlockSpec((HI, 1, PL, N), lambda c: (0, c, 0, 0))],
        out_specs=pl.BlockSpec((1,) + shape[1:], lambda c: (c, 0, 0, 0, 0)),
        out_shape=jax.ShapeDtypeStruct(shape, jnp.float32),
        compiler_params=pltpu.CompilerParams(vmem_limit_bytes=60 << 20),
        cost_estimate=pl.CostEstimate(flops=0, bytes_accessed=7 << 20, transcendentals=0),
        name="choose_phases",
    )(turned)


def turn_kernel(phase_ref, order_ref, cos_ref, sin_ref, cos0_ref, sin0_ref, lowest_ref):
    for j in range(GX):
        for s in range(HI // ROWS):
            start = j * HI + s * ROWS
            at = pl.ds(start, ROWS)
            angles = phase_ref[j, s, :ROWS].reshape(ROWS * SLOTS, N)
            high = angles.astype(jnp.bfloat16)
            rest = angles - high.astype(jnp.float32)
            mid = rest.astype(jnp.bfloat16)
            low = (rest - mid.astype(jnp.float32)).astype(jnp.bfloat16)
            angles = dot(jnp.concatenate([high, mid, low], axis=1), order_ref[...])
            cos_ref[at] = jnp.cos(angles).reshape(ROWS, SLOTS, N)
            sin_ref[at] = jnp.sin(angles).reshape(ROWS, SLOTS, N)
            first = phase_ref[j, s, :ROWS, 0, :N // 2]
            cos0_ref[at, :] = jnp.cos(first)
            sin0_ref[at, :] = jnp.sin(first)
            tail = phase_ref[j, s, ROWS]
            lowest_ref[pl.ds(start, 8), :] = tail[:, :N // 2]
            lowest_ref[pl.ds(start + 8, 8), :] = tail[:, N // 2:]


def turn_factors(phases, order):
    whole = pl.BlockSpec(memory_space=pltpu.VMEM)
    full = jax.ShapeDtypeStruct((N, SLOTS, N), jnp.float32)
    first = jax.ShapeDtypeStruct((N, N // 2), jnp.float32)
    return pl.pallas_call(
        turn_kernel,
        in_specs=[whole] * 2,
        out_specs=[whole] * 5,
        out_shape=[full, full, first, first, first],
        compiler_params=pltpu.CompilerParams(vmem_limit_bytes=24 << 20),
        cost_estimate=pl.CostEstimate(flops=0, bytes_accessed=8 << 20, transcendentals=2 * N * N * SLOTS),
        name="turn_factors",
    )(phases, order)


def middle_kernel(r_hbm, cos_hbm, sin_hbm, cos0_hbm, sin0_hbm, lowest_hbm, tables_hbm, shift_ref, fraction_ref,
                  y_hbm, buf, xa, xb, xc, cos_ref, sin_ref, cos0_ref, sin0_ref, cos1_ref, sin1_ref, tables_ref,
                  bits_ref, w_ref, s_ref, block_sems, sems):
    half = N // 2
    special = lax.axis_index("pa") == 0
    inbound = [pltpu.make_async_copy(r_hbm.at[a], buf.at[a], block_sems.at[a]) for a in range(GX)]
    extras = [
        pltpu.make_async_copy(source, target, sems.at[n])
        for n, (source, target) in enumerate((
            (tables_hbm, tables_ref), (cos_hbm, cos_ref), (sin_hbm, sin_ref),
            (cos0_hbm, cos0_ref), (sin0_hbm, sin0_ref), (lowest_hbm, cos1_ref),
        ))
    ]
    for copy in inbound + extras:
        copy.start()
    fe_ref, fo_ref, ie_ref, io_ref, fr_ref, ir_ref = (tables_ref.at[n] for n in range(6))

    steps = jnp.broadcast_to(shift_ref[...], (8, N)) + SMAX
    for bit in range(5):
        bits_ref[bit] = (steps >> bit) & 1
    for k, weight in enumerate(cubic_weights(jnp.broadcast_to(fraction_ref[...], (8, N)))):
        w_ref[k] = weight
    block_ids = lax.broadcasted_iota(jnp.int32, (8, 128), 1) // PL

    def gather(a, g, carry):
        step = a * 4 + g
        lane = pl.multiple_of(g * 128, 128)
        row = PAD_LO + step * 8
        for mh in range(2):
            for bh in range(2):
                pieces = [buf[a, bh * 8 + j, mh * 8:mh * 8 + 8, pl.ds(lane, 128)] for j in range(8)]
                pieces = deal(pieces, block_ids)
                for j in range(8):
                    piece = pltpu.roll(pieces[j], 128 - PL * j, 1) if j else pieces[j]
                    xa[bh, row + j, mh * 8:mh * 8 + 8, :] = piece
        return carry

    def wrap(x):
        x[:, 0:PAD_LO] = x[:, N:N + PAD_LO]
        x[:, PAD_LO + N:PAD_LO + N + PAD_HI] = x[:, PAD_LO:PAD_LO + PAD_HI]

    def drift(x, first):
        need = TILE + 3
        for mh in range(2):
            for ph in range(2):
                ms = slice(mh * 8, mh * 8 + 8)
                ps = slice(ph * 128, ph * 128 + 128)
                rows = need + 31
                z = x[ph, pl.ds(first + PAD_LO + SMAX - 1 - 31, rows), ms, :]
                for bit in (4, 3, 2, 1, 0):
                    size = 1 << bit
                    taken = bits_ref[bit, :, ps] != 0
                    z = jnp.where(taken[None], z[:rows - size], z[size:])
                    rows = rows - size
                total = w_ref[0, :, ps][None] * z[0:TILE]
                for k in (1, 2, 3):
                    total = total + w_ref[k, :, ps][None] * z[k:k + TILE]
                xb[ph, pl.ds(first, TILE), ms, :] = total

    def turned(y, c, s, forward_ref, inverse_ref):
        z = dot(parts_of(y), forward_ref[...])
        zr, zi = z[:, :half], z[:, half:]
        g = jnp.concatenate([zr * c - zi * s, zr * s + zi * c], axis=1)
        return dot(parts_of(g), inverse_ref[...])

    def kick(to_ref, first):
        rows = KTILE * SLOTS
        at = pl.ds(first, KTILE)
        low, high = (
            jnp.concatenate([xb[h, at, m:m + 8, :].reshape(rows, half) for m in (0, 8)], axis=1)
            for h in range(2)
        )
        cos = cos_ref[at].reshape(rows, N)
        sin = sin_ref[at].reshape(rows, N)
        even = turned(low + high, cos[:, :half], sin[:, :half], fe_ref, ie_ref)
        odd = turned(low - high, cos[:, half:], sin[:, half:], fo_ref, io_ref)
        out = pl.ds(first + PAD_LO, KTILE)
        for h, both in enumerate((even + odd, even - odd)):
            to_ref[h, out, 0:8, :] = both[:, :half].reshape(KTILE, 8, half)
            to_ref[h, out, 8:16, :] = both[:, half:].reshape(KTILE, 8, half)

    def shared_slot():
        flat = xb.reshape(2 * N * M, half)
        x = jnp.concatenate([
            jnp.concatenate([flat[pl.ds(h * N * M + row, N, stride=M), :] for h in range(2)], axis=1)
            for row in (0, SLOTS)
        ], axis=0)
        c = jnp.concatenate([cos0_ref[...], cos1_ref[...]], axis=0)
        s = jnp.concatenate([sin0_ref[...], sin1_ref[...]], axis=0)
        s_ref[...] = turned(x, c, s, fr_ref, ir_ref)

    def place_shared(to_ref, first, count):
        flat = to_ref.reshape(2 * to_ref.shape[1] * M, half)
        for h in range(2):
            for part in range(2):
                start = (h * to_ref.shape[1] + PAD_LO + first) * M + part * SLOTS
                flat[pl.ds(start, count, stride=M), :] = s_ref[part * N + first:part * N + first + count,
                                                               h * half:h * half + half]

    def scatter(a, g):
        lane = g * 128
        row = PAD_LO + a * HI + g * 8
        for mh in range(2):
            for bh in range(2):
                pieces = [xa[bh, row + j, mh * 8:mh * 8 + 8, :] for j in range(8)]
                pieces = [pltpu.roll(pieces[j], PL * j, 1) if j else pieces[j] for j in range(8)]
                pieces = deal(pieces, block_ids)
                for j in range(8):
                    buf[a, bh * 8 + j, mh * 8:mh * 8 + 8, lane:lane + 128] = pieces[j]

    def drift_tile(x, tile):
        for part in range(KTILE // TILE):
            drift(x, tile * KTILE + part * TILE)

    for a in range(GX):
        inbound[a].wait()
        lax.fori_loop(0, HI // 8, functools.partial(gather, a), 0, unroll=2)
    tiles = N // KTILE
    done = (tiles - 1) * KTILE
    outbound = [pltpu.make_async_copy(buf.at[a], y_hbm.at[a], block_sems.at[a]) for a in range(GX)]
    for substep in range(STEPS):
        source, target = (xa, xc) if substep % 2 == 0 else (xc, xa)
        last = substep + 1 == STEPS
        wrap(source)
        drift_tile(source, 0)
        if substep == 0:
            for copy in extras:
                copy.wait()

            @pl.when(special)
            def _():
                angles = cos1_ref[...]
                cos1_ref[...] = jnp.cos(angles)
                sin1_ref[...] = jnp.sin(angles)

        for tile in range(tiles - 1):
            drift_tile(source, tile + 1)
            kick(target, tile * KTILE)

        @pl.when(special)
        def _():
            shared_slot()
            if last:
                place_shared(target, 0, done)

        kick(target, done)
        if last:
            for a in range(done // HI):
                for g in range(HI // 8):
                    scatter(a, g)
                outbound[a].start()

        @pl.when(special)
        def _():
            if last:
                place_shared(target, done, KTILE)
            else:
                place_shared(target, 0, N)

    for a in range(done // HI, GX):
        for g in range(HI // 8):
            scatter(a, g)
        outbound[a].start()
    for copy in outbound:
        copy.wait()


def middle(received, factors, lowest, tables, shifts, fractions):
    anywhere = pl.BlockSpec(memory_space=pl.ANY)
    whole = pl.BlockSpec(memory_space=pltpu.VMEM)
    return pl.pallas_call(
        middle_kernel,
        in_specs=[anywhere] * 7 + [whole] * 2,
        out_specs=anywhere,
        out_shape=jax.ShapeDtypeStruct((GX, PA, M, LANES), jnp.float32),
        scratch_shapes=[
            pltpu.VMEM((GX, PA, M, LANES), jnp.float32),
            pltpu.VMEM((2, PAD_LO + N + PAD_HI, M, N // 2), jnp.float32),
            pltpu.VMEM((2, N, M, N // 2), jnp.float32),
            pltpu.VMEM((2, PAD_LO + N + PAD_HI, M, N // 2), jnp.float32),
            pltpu.VMEM((N, SLOTS, N), jnp.float32),
            pltpu.VMEM((N, SLOTS, N), jnp.float32),
        ] + [pltpu.VMEM((N, N // 2), jnp.float32)] * 4 + [
            pltpu.VMEM((6, 3 * N, N), jnp.bfloat16),
            pltpu.VMEM((5, 8, N), jnp.int32),
            pltpu.VMEM((4, 8, N), jnp.float32),
            pltpu.VMEM((2 * N, N), jnp.float32),
            pltpu.SemaphoreType.DMA((GX,)),
            pltpu.SemaphoreType.DMA((6,)),
        ],
        compiler_params=pltpu.CompilerParams(vmem_limit_bytes=60 << 20),
        cost_estimate=pl.CostEstimate(flops=24 * 2048 * 2 * N * N, bytes_accessed=14 << 20, transcendentals=0),
        name="middle",
    )(received, *factors, lowest, tables, shifts, fractions)


def cubic_weights(fraction):
    return (
        -fraction * (fraction - 1.0) * (fraction - 2.0) / 6.0,
        (fraction + 1.0) * (fraction - 1.0) * (fraction - 2.0) / 2.0,
        -(fraction + 1.0) * fraction * (fraction - 2.0) / 2.0,
        (fraction + 1.0) * fraction * (fraction - 1.0) / 6.0,
    )


def shards(density, shifts, fractions, kick_phase):
    forward, inverse = (jnp.asarray(t) for t in second_tables())
    (fe, ie), (fo, io), (fr, ir) = paired(True), paired(False), real_tables()
    tables = jnp.asarray(np.stack([fe, fo, ie, io, fr, ir]))
    chosen = choose_phases(kick_phase.transpose(0, 2, 3, 1))
    chosen, density = lax.optimization_barrier((chosen, density))
    phases = lax.all_to_all(chosen, "gx", 0, 0, tiled=True)
    spectral = forward_second(density, forward).reshape(GX * PA, M, LANES)
    phases, spectral = lax.optimization_barrier((phases, spectral))
    received = lax.all_to_all(spectral, ("gx", "pa"), 0, 0, tiled=True)
    received = received.reshape(GX, PA, M, LANES)
    *factors, lowest = turn_factors(phases, jnp.asarray(parity_order()))
    lowest = lax.ppermute(lowest, "pa", [(PA // 2, 0)])
    sent = middle(received, factors, lowest, tables, shifts.reshape(1, N), fractions.reshape(1, N))
    sent = sent.reshape(GX * PA, M, LANES)
    returned = lax.all_to_all(sent, ("gx", "pa"), 0, 0, tiled=True)
    return inverse_second(returned.reshape(GX, N, LANES), inverse)


def solution(mesh):
    placed = (P("gx", "pa", None, None), P(), P(), P("gx", None, None, "pa"))
    return jax.shard_map(
        shards, mesh=mesh, in_specs=placed, out_specs=P("gx", "pa", None, None), check_vma=False
    )
```

```python
import functools
import math

import jax
import jax.numpy as jnp
import ml_dtypes
import numpy as np
from jax import lax
from jax.experimental import pallas as pl
from jax.experimental.pallas import tpu as pltpu
from jax.sharding import PartitionSpec as P

STEPS = 2
N = 256
GX = 8
PA = 16
HI = N // GX
PL = N // PA
SLOTS = 8
M = 2 * SLOTS
LANES = HI * PL
PAD_LO = 24
PAD_HI = 16
SMAX = 10
TILE = 32
KTILE = 64
ROWS = 16


def split_table(table):
    high = table.astype(ml_dtypes.bfloat16)
    low = (table - high.astype(np.float64)).astype(ml_dtypes.bfloat16)
    return high, low


def stacked(table):
    high, low = split_table(table)
    return np.concatenate([high, high, low], axis=0)


def owned_columns(device):
    start = PL * device + (0 if device < PA // 2 else 1)
    return [start + slot for slot in range(SLOTS)]


def second_tables():
    q = np.arange(N)
    forward = np.zeros((N, N))
    inverse = np.zeros((N, N))
    scale = 1.0 / N ** (STEPS + 1)
    for device in range(PA):
        for slot, col in enumerate(owned_columns(device)):
            angle = 2.0 * math.pi * (q * col % N) / N
            re_row = device * M + slot
            im_row = re_row + SLOTS
            if col == 0:
                half = 1.0 - 2.0 * (q % 2)
                forward[:, re_row] = 1.0
                forward[:, im_row] = half
                inverse[re_row] = scale
                inverse[im_row] = scale * half
            else:
                forward[:, re_row] = np.cos(angle)
                forward[:, im_row] = -np.sin(angle)
                inverse[re_row] = 2.0 * scale * np.cos(angle)
                inverse[im_row] = -2.0 * scale * np.sin(angle)
    return stacked(forward), stacked(inverse)


def paired(even):
    half = np.arange(N // 2)
    k = 2 * half + (0 if even else 1)
    angle = 2.0 * math.pi * (half[:, None] * k[None, :] % N) / N
    cos, sin = np.cos(angle), np.sin(angle)
    forward = np.block([[cos, -sin], [sin, cos]])
    inverse = np.block([[cos.T, sin.T], [-sin.T, cos.T]])
    return stacked(forward), stacked(inverse)


def real_tables():
    p = np.arange(N)
    k = np.arange(N // 2)
    angle = 2.0 * math.pi * (p[:, None] * k[None, :] % N) / N
    last = (1.0 - 2.0 * (p % 2))[:, None]
    cos, sin = np.cos(angle), np.sin(angle)
    forward = np.concatenate([cos, last, -sin[:, 1:]], axis=1)
    inverse = np.concatenate([cos[:, :1], 2.0 * cos[:, 1:], last, -2.0 * sin[:, 1:]], axis=1).T
    return stacked(forward), stacked(inverse)


def parity_order():
    table = np.zeros((N, N))
    k = np.concatenate([np.arange(0, N, 2), np.arange(1, N, 2)])
    table[k, np.arange(N)] = 1.0
    return np.concatenate([table] * 3, axis=0).astype(ml_dtypes.bfloat16)


def parts_of(values):
    high = values.astype(jnp.bfloat16)
    low = (values - high.astype(jnp.float32)).astype(jnp.bfloat16)
    return jnp.concatenate([high, low, high], axis=1)


def dot(a, b):
    return jnp.dot(a, b, preferred_element_type=jnp.float32)


def forward_kernel(low_ref, high_ref, table_ref, out_ref):
    low = low_ref.reshape(8 * PL * GX, N // 2)
    high = high_ref.reshape(8 * PL * GX, N // 2)
    rank = lax.axis_index("pa")
    for c in range(GX):
        rows = []
        for n in range(8):
            at = pl.ds((n + PA - rank) % 8 * (PL * GX) + c, PL, stride=GX)
            rows.append(jnp.concatenate([low[at, :], high[at, :]], axis=1))
        rows = jnp.concatenate(rows, axis=0)
        out_ref[c] = dot(parts_of(rows), table_ref[...]).T


def forward_second(density, table):
    return pl.pallas_call(
        forward_kernel,
        grid=(HI // 8,),
        in_specs=[
            pl.BlockSpec((8, PL, GX, N // 2), lambda s: (s, 0, 0, 0)),
            pl.BlockSpec((8, PL, GX, N // 2), lambda s: (s, 0, 0, 1)),
            pl.BlockSpec((3 * N, N), lambda s: (0, 0)),
        ],
        out_specs=pl.BlockSpec((GX, N, 8 * PL), lambda s: (0, 0, s)),
        out_shape=jax.ShapeDtypeStruct((GX, N, LANES), jnp.float32),
        compiler_params=pltpu.CompilerParams(vmem_limit_bytes=60 << 20),
        cost_estimate=pl.CostEstimate(flops=6 * 4096 * N * N, bytes_accessed=9 << 20, transcendentals=0),
        name="forward_second",
    )(density, density, table)


def inverse_kernel(v_ref, table_ref, out_ref):
    rank = lax.axis_index("pa")
    for c in range(GX):
        rows = dot(parts_of(v_ref[c].T), table_ref[...]).reshape(8, PL, N)
        for n in range(8):
            out_ref[(n + PA - rank) % 8, :, c, :] = rows[n]


def inverse_second(spectral, table):
    return pl.pallas_call(
        inverse_kernel,
        grid=(HI // 8,),
        in_specs=[
            pl.BlockSpec((GX, N, 8 * PL), lambda s: (0, 0, s)),
            pl.BlockSpec((3 * N, N), lambda s: (0, 0)),
        ],
        out_specs=pl.BlockSpec((8, PL, GX, N), lambda s: (s, 0, 0, 0)),
        out_shape=jax.ShapeDtypeStruct((HI, PL, GX, N), jnp.float32),
        compiler_params=pltpu.CompilerParams(vmem_limit_bytes=32 << 20),
        cost_estimate=pl.CostEstimate(flops=6 * 4096 * N * N, bytes_accessed=9 << 20, transcendentals=0),
        name="inverse_second",
    )(spectral, table)


def deal(pieces, block_ids):
    pieces = [pieces[-d % 8] for d in range(8)]
    for step in (1, 2, 4):
        taken = (block_ids & step) != 0
        pieces = [jnp.where(taken, pieces[(d - step) % 8], pieces[d]) for d in range(8)]
    return pieces


def choose_kernel(phase_ref, out_ref):
    low = lax.axis_index("pa") < PA // 2
    for c in range(GX):
        out_ref[c, 0, :ROWS] = jnp.where(low, phase_ref[:, c, 0:SLOTS, :], phase_ref[:, c, 1:SLOTS + 1, :])
        first = phase_ref[:, c, 0, :N // 2]
        out_ref[c, 0, ROWS] = jnp.concatenate([first[:8], first[8:]], axis=1)


def choose_phases(turned):
    shape = (GX, HI // ROWS, ROWS + 1, SLOTS, N)
    return pl.pallas_call(
        choose_kernel,
        grid=(HI // ROWS,),
        in_specs=[pl.BlockSpec((ROWS, GX, PL, N), lambda s: (s, 0, 0, 0))],
        out_specs=pl.BlockSpec((GX, 1) + shape[2:], lambda s: (0, s, 0, 0, 0)),
        out_shape=jax.ShapeDtypeStruct(shape, jnp.float32),
        compiler_params=pltpu.CompilerParams(vmem_limit_bytes=60 << 20),
        cost_estimate=pl.CostEstimate(flops=0, bytes_accessed=7 << 20, transcendentals=0),
        name="choose_phases",
    )(turned)


def turn_kernel(phase_ref, order_ref, cos_ref, sin_ref, cos0_ref, sin0_ref, lowest_ref):
    for j in range(GX):
        for s in range(HI // ROWS):
            start = j * HI + s * ROWS
            at = pl.ds(start, ROWS)
            angles = phase_ref[j, s, :ROWS].reshape(ROWS * SLOTS, N)
            high = angles.astype(jnp.bfloat16)
            rest = angles - high.astype(jnp.float32)
            mid = rest.astype(jnp.bfloat16)
            low = (rest - mid.astype(jnp.float32)).astype(jnp.bfloat16)
            angles = dot(jnp.concatenate([high, mid, low], axis=1), order_ref[...])
            cos_ref[at] = jnp.cos(angles).reshape(ROWS, SLOTS, N)
            sin_ref[at] = jnp.sin(angles).reshape(ROWS, SLOTS, N)
            first = phase_ref[j, s, :ROWS, 0, :N // 2]
            cos0_ref[at, :] = jnp.cos(first)
            sin0_ref[at, :] = jnp.sin(first)
            tail = phase_ref[j, s, ROWS]
            for n, turn in enumerate((jnp.cos(tail), jnp.sin(tail))):
                lowest_ref[n, pl.ds(start, 8), :] = turn[:, :N // 2]
                lowest_ref[n, pl.ds(start + 8, 8), :] = turn[:, N // 2:]


def turn_factors(phases, order):
    whole = pl.BlockSpec(memory_space=pltpu.VMEM)
    full = jax.ShapeDtypeStruct((N, SLOTS, N), jnp.float32)
    first = jax.ShapeDtypeStruct((N, N // 2), jnp.float32)
    return pl.pallas_call(
        turn_kernel,
        in_specs=[whole] * 2,
        out_specs=[whole] * 5,
        out_shape=[full, full, first, first, jax.ShapeDtypeStruct((2, N, N // 2), jnp.float32)],
        compiler_params=pltpu.CompilerParams(vmem_limit_bytes=24 << 20),
        cost_estimate=pl.CostEstimate(flops=0, bytes_accessed=8 << 20, transcendentals=2 * N * N * SLOTS),
        name="turn_factors",
    )(phases, order)


def middle_kernel(r_hbm, cos_hbm, sin_hbm, cos0_hbm, sin0_hbm, lowest_hbm, tables_hbm, shift_ref, fraction_ref,
                  y_hbm, buf, xa, xb, xc, cos_ref, sin_ref, cos0_ref, sin0_ref, turn1_ref, tables_ref,
                  bits_ref, w_ref, s_ref, block_sems, sems):
    half = N // 2
    special = lax.axis_index("pa") == 0
    inbound = [pltpu.make_async_copy(r_hbm.at[a], buf.at[a], block_sems.at[a]) for a in range(GX)]
    extras = [
        pltpu.make_async_copy(source, target, sems.at[n])
        for n, (source, target) in enumerate((
            (tables_hbm, tables_ref), (cos_hbm, cos_ref), (sin_hbm, sin_ref),
            (cos0_hbm, cos0_ref), (sin0_hbm, sin0_ref), (lowest_hbm, turn1_ref),
        ))
    ]
    for copy in inbound + extras:
        copy.start()
    fe_ref, fo_ref, ie_ref, io_ref, fr_ref, ir_ref = (tables_ref.at[n] for n in range(6))

    steps = jnp.broadcast_to(shift_ref[...], (8, N)) + SMAX
    for bit in range(5):
        bits_ref[bit] = (steps >> bit) & 1
    for k, weight in enumerate(cubic_weights(jnp.broadcast_to(fraction_ref[...], (8, N)))):
        w_ref[k] = weight
    block_ids = lax.broadcasted_iota(jnp.int32, (8, 128), 1) // PL

    def gather(a, g, carry):
        step = a * 4 + g
        lane = pl.multiple_of(g * 128, 128)
        row = PAD_LO + step * 8
        for mh in range(2):
            for bh in range(2):
                pieces = [buf[a, bh * 8 + j, mh * 8:mh * 8 + 8, pl.ds(lane, 128)] for j in range(8)]
                pieces = deal(pieces, block_ids)
                for j in range(8):
                    piece = pltpu.roll(pieces[j], 128 - PL * j, 1) if j else pieces[j]
                    xa[bh, row + j, mh * 8:mh * 8 + 8, :] = piece
        return carry

    def wrap(x):
        x[:, 0:PAD_LO] = x[:, N:N + PAD_LO]
        x[:, PAD_LO + N:PAD_LO + N + PAD_HI] = x[:, PAD_LO:PAD_LO + PAD_HI]

    def drift(x, first):
        need = TILE + 3
        for mh in range(2):
            for ph in range(2):
                ms = slice(mh * 8, mh * 8 + 8)
                ps = slice(ph * 128, ph * 128 + 128)
                rows = need + 31
                z = x[ph, pl.ds(first + PAD_LO + SMAX - 1 - 31, rows), ms, :]
                for bit in (4, 3, 2, 1, 0):
                    size = 1 << bit
                    taken = bits_ref[bit, :, ps] != 0
                    z = jnp.where(taken[None], z[:rows - size], z[size:])
                    rows = rows - size
                total = w_ref[0, :, ps][None] * z[0:TILE]
                for k in (1, 2, 3):
                    total = total + w_ref[k, :, ps][None] * z[k:k + TILE]
                xb[ph, pl.ds(first, TILE), ms, :] = total

    def turned(y, c, s, forward_ref, inverse_ref):
        z = dot(parts_of(y), forward_ref[...])
        zr, zi = z[:, :half], z[:, half:]
        g = jnp.concatenate([zr * c - zi * s, zr * s + zi * c], axis=1)
        return dot(parts_of(g), inverse_ref[...])

    def kick(to_ref, first):
        rows = KTILE * SLOTS
        at = pl.ds(first, KTILE)
        low, high = (
            jnp.concatenate([xb[h, at, m:m + 8, :].reshape(rows, half) for m in (0, 8)], axis=1)
            for h in range(2)
        )
        cos = cos_ref[at].reshape(rows, N)
        sin = sin_ref[at].reshape(rows, N)
        even = turned(low + high, cos[:, :half], sin[:, :half], fe_ref, ie_ref)
        odd = turned(low - high, cos[:, half:], sin[:, half:], fo_ref, io_ref)
        out = pl.ds(first + PAD_LO, KTILE)
        for h, both in enumerate((even + odd, even - odd)):
            to_ref[h, out, 0:8, :] = both[:, :half].reshape(KTILE, 8, half)
            to_ref[h, out, 8:16, :] = both[:, half:].reshape(KTILE, 8, half)

    def shared_slot():
        flat = xb.reshape(2 * N * M, half)
        x = jnp.concatenate([
            jnp.concatenate([flat[pl.ds(h * N * M + row, N, stride=M), :] for h in range(2)], axis=1)
            for row in (0, SLOTS)
        ], axis=0)
        c = jnp.concatenate([cos0_ref[...], turn1_ref[0]], axis=0)
        s = jnp.concatenate([sin0_ref[...], turn1_ref[1]], axis=0)
        s_ref[...] = turned(x, c, s, fr_ref, ir_ref)

    def place_shared(to_ref, first, count):
        flat = to_ref.reshape(2 * to_ref.shape[1] * M, half)
        for h in range(2):
            for part in range(2):
                start = (h * to_ref.shape[1] + PAD_LO + first) * M + part * SLOTS
                flat[pl.ds(start, count, stride=M), :] = s_ref[part * N + first:part * N + first + count,
                                                               h * half:h * half + half]

    def scatter(a, g):
        lane = g * 128
        row = PAD_LO + a * HI + g * 8
        for mh in range(2):
            for bh in range(2):
                pieces = [xa[bh, row + j, mh * 8:mh * 8 + 8, :] for j in range(8)]
                pieces = [pltpu.roll(pieces[j], PL * j, 1) if j else pieces[j] for j in range(8)]
                pieces = deal(pieces, block_ids)
                for j in range(8):
                    buf[a, bh * 8 + j, mh * 8:mh * 8 + 8, lane:lane + 128] = pieces[j]

    def drift_tile(x, tile):
        for part in range(KTILE // TILE):
            drift(x, tile * KTILE + part * TILE)

    for a in range(GX):
        inbound[a].wait()
        lax.fori_loop(0, HI // 8, functools.partial(gather, a), 0, unroll=2)
    tiles = N // KTILE
    done = (tiles - 1) * KTILE
    outbound = [pltpu.make_async_copy(buf.at[a], y_hbm.at[a], block_sems.at[a]) for a in range(GX)]
    for substep in range(STEPS):
        source, target = (xa, xc) if substep % 2 == 0 else (xc, xa)
        last = substep + 1 == STEPS
        wrap(source)
        drift_tile(source, 0)
        if substep == 0:
            for copy in extras:
                copy.wait()

        for tile in range(tiles - 1):
            drift_tile(source, tile + 1)
            if tile == tiles - 2:
                shared_slot()
            kick(target, tile * KTILE)

        if last:
            @pl.when(special)
            def _():
                place_shared(target, 0, done)

        kick(target, done)
        if last:
            for a in range(done // HI):
                for g in range(HI // 8):
                    scatter(a, g)
                outbound[a].start()

        @pl.when(special)
        def _():
            if last:
                place_shared(target, done, KTILE)
            else:
                place_shared(target, 0, N)

    for a in range(done // HI, GX):
        for g in range(HI // 8):
            scatter(a, g)
        outbound[a].start()
    for copy in outbound:
        copy.wait()


def middle(received, factors, lowest, tables, shifts, fractions):
    anywhere = pl.BlockSpec(memory_space=pl.ANY)
    whole = pl.BlockSpec(memory_space=pltpu.VMEM)
    return pl.pallas_call(
        middle_kernel,
        in_specs=[anywhere] * 7 + [whole] * 2,
        out_specs=anywhere,
        out_shape=jax.ShapeDtypeStruct((GX, PA, M, LANES), jnp.float32),
        scratch_shapes=[
            pltpu.VMEM((GX, PA, M, LANES), jnp.float32),
            pltpu.VMEM((2, PAD_LO + N + PAD_HI, M, N // 2), jnp.float32),
            pltpu.VMEM((2, N, M, N // 2), jnp.float32),
            pltpu.VMEM((2, PAD_LO + N + PAD_HI, M, N // 2), jnp.float32),
            pltpu.VMEM((N, SLOTS, N), jnp.float32),
            pltpu.VMEM((N, SLOTS, N), jnp.float32),
        ] + [pltpu.VMEM((N, N // 2), jnp.float32)] * 2 + [
            pltpu.VMEM((2, N, N // 2), jnp.float32),
            pltpu.VMEM((6, 3 * N, N), jnp.bfloat16),
            pltpu.VMEM((5, 8, N), jnp.int32),
            pltpu.VMEM((4, 8, N), jnp.float32),
            pltpu.VMEM((2 * N, N), jnp.float32),
            pltpu.SemaphoreType.DMA((GX,)),
            pltpu.SemaphoreType.DMA((6,)),
        ],
        compiler_params=pltpu.CompilerParams(vmem_limit_bytes=60 << 20),
        cost_estimate=pl.CostEstimate(flops=24 * 2048 * 2 * N * N, bytes_accessed=14 << 20, transcendentals=0),
        name="middle",
    )(received, *factors, lowest, tables, shifts, fractions)


def cubic_weights(fraction):
    return (
        -fraction * (fraction - 1.0) * (fraction - 2.0) / 6.0,
        (fraction + 1.0) * (fraction - 1.0) * (fraction - 2.0) / 2.0,
        -(fraction + 1.0) * fraction * (fraction - 2.0) / 2.0,
        (fraction + 1.0) * fraction * (fraction - 1.0) / 6.0,
    )


def shards(density, shifts, fractions, kick_phase):
    forward, inverse = (jnp.asarray(t) for t in second_tables())
    (fe, ie), (fo, io), (fr, ir) = paired(True), paired(False), real_tables()
    tables = jnp.asarray(np.stack([fe, fo, ie, io, fr, ir]))
    chosen = choose_phases(kick_phase.transpose(0, 2, 3, 1))
    chosen, density = lax.optimization_barrier((chosen, density))
    phases = lax.all_to_all(chosen, "gx", 0, 0, tiled=True)
    spectral = forward_second(density, forward).reshape(GX * PA, M, LANES)
    phases, spectral = lax.optimization_barrier((phases, spectral))
    received = lax.all_to_all(spectral, ("gx", "pa"), 0, 0, tiled=True)
    received = received.reshape(GX, PA, M, LANES)
    *factors, lowest = turn_factors(phases, jnp.asarray(parity_order()))
    lowest = lax.ppermute(lowest, "pa", [(PA // 2, 0)])
    sent = middle(received, factors, lowest, tables, shifts.reshape(1, N), fractions.reshape(1, N))
    sent = sent.reshape(GX * PA, M, LANES)
    returned = lax.all_to_all(sent, ("gx", "pa"), 0, 0, tiled=True)
    return inverse_second(returned.reshape(GX, N, LANES), inverse)


def solution(mesh):
    placed = (P("gx", "pa", None, None), P(), P(), P("gx", None, None, "pa"))
    return jax.shard_map(
        shards, mesh=mesh, in_specs=placed, out_specs=P("gx", "pa", None, None), check_vma=False
    )
```

```python
import functools
import math

import jax
import jax.numpy as jnp
import ml_dtypes
import numpy as np
from jax import lax
from jax.experimental import pallas as pl
from jax.experimental.pallas import tpu as pltpu
from jax.sharding import PartitionSpec as P

STEPS = 2
N = 256
GX = 8
PA = 16
HI = N // GX
PL = N // PA
SLOTS = 8
M = 2 * SLOTS
LANES = HI * PL
PAD_LO = 24
PAD_HI = 16
SMAX = 10
TILE = 32
KTILE = 64
ROWS = 16


def split_table(table):
    high = table.astype(ml_dtypes.bfloat16)
    low = (table - high.astype(np.float64)).astype(ml_dtypes.bfloat16)
    return high, low


def stacked(table):
    high, low = split_table(table)
    return np.concatenate([high, high, low], axis=0)


def both_parts(table):
    return np.concatenate(split_table(table), axis=0)


def owned_columns(device):
    start = PL * device
    return [start + (0 if device < PA // 2 else SLOTS)] + [start + slot for slot in range(1, SLOTS)]


def second_tables():
    q = np.arange(N)
    forward = np.zeros((N, N))
    inverse = np.zeros((N, N))
    scale = 1.0 / N ** (STEPS + 1)
    for device in range(PA):
        for slot, col in enumerate(owned_columns(device)):
            angle = 2.0 * math.pi * (q * col % N) / N
            re_row = device * M + slot
            im_row = re_row + SLOTS
            if col == 0:
                half = 1.0 - 2.0 * (q % 2)
                forward[:, re_row] = 1.0
                forward[:, im_row] = half
                inverse[re_row] = scale
                inverse[im_row] = scale * half
            else:
                forward[:, re_row] = np.cos(angle)
                forward[:, im_row] = -np.sin(angle)
                inverse[re_row] = 2.0 * scale * np.cos(angle)
                inverse[im_row] = -2.0 * scale * np.sin(angle)
    return stacked(forward), stacked(inverse)


def paired(even):
    half = np.arange(N // 2)
    k = 2 * half + (0 if even else 1)
    angle = 2.0 * math.pi * (half[:, None] * k[None, :] % N) / N
    cos, sin = np.cos(angle), np.sin(angle)
    forward = np.block([[cos, -sin], [sin, cos]])
    inverse = np.block([[cos.T, sin.T], [-sin.T, cos.T]])
    return both_parts(forward), both_parts(inverse)


def real_tables():
    p = np.arange(N)
    k = np.arange(N // 2)
    angle = 2.0 * math.pi * (p[:, None] * k[None, :] % N) / N
    last = (1.0 - 2.0 * (p % 2))[:, None]
    cos, sin = np.cos(angle), np.sin(angle)
    forward = np.concatenate([cos, last, -sin[:, 1:]], axis=1)
    inverse = np.concatenate([cos[:, :1], 2.0 * cos[:, 1:], last, -2.0 * sin[:, 1:]], axis=1).T
    return both_parts(forward), both_parts(inverse)


def parity_order():
    table = np.zeros((N, N))
    k = np.concatenate([np.arange(0, N, 2), np.arange(1, N, 2)])
    table[k, np.arange(N)] = 1.0
    return np.concatenate([table] * 3, axis=0).astype(ml_dtypes.bfloat16)


def parts_of(values):
    high = values.astype(jnp.bfloat16)
    low = (values - high.astype(jnp.float32)).astype(jnp.bfloat16)
    return jnp.concatenate([high, low, high], axis=1)


def dot(a, b):
    return jnp.dot(a, b, preferred_element_type=jnp.float32)


def three_dots(values, table_ref):
    high = values.astype(jnp.bfloat16)
    low = (values - high.astype(jnp.float32)).astype(jnp.bfloat16)
    top = table_ref[:N]
    return dot(high, top) + dot(low, top) + dot(high, table_ref[N:])


def forward_kernel(low_ref, high_ref, table_ref, out_ref):
    low = low_ref.reshape(8 * PL * GX, N // 2)
    high = high_ref.reshape(8 * PL * GX, N // 2)
    rank = lax.axis_index("pa")
    for c in range(GX):
        rows = []
        for n in range(8):
            at = pl.ds((n + PA - rank) % 8 * (PL * GX) + c, PL, stride=GX)
            rows.append(jnp.concatenate([low[at, :], high[at, :]], axis=1))
        rows = jnp.concatenate(rows, axis=0)
        out_ref[c] = dot(parts_of(rows), table_ref[...]).T


def forward_second(density, table):
    return pl.pallas_call(
        forward_kernel,
        grid=(HI // 8,),
        in_specs=[
            pl.BlockSpec((8, PL, GX, N // 2), lambda s: (s, 0, 0, 0)),
            pl.BlockSpec((8, PL, GX, N // 2), lambda s: (s, 0, 0, 1)),
            pl.BlockSpec((3 * N, N), lambda s: (0, 0)),
        ],
        out_specs=pl.BlockSpec((GX, N, 8 * PL), lambda s: (0, 0, s)),
        out_shape=jax.ShapeDtypeStruct((GX, N, LANES), jnp.float32),
        compiler_params=pltpu.CompilerParams(vmem_limit_bytes=60 << 20),
        cost_estimate=pl.CostEstimate(flops=6 * 4096 * N * N, bytes_accessed=9 << 20, transcendentals=0),
        name="forward_second",
    )(density, density, table)


def inverse_kernel(v_ref, table_ref, out_ref):
    rank = lax.axis_index("pa")
    for c in range(GX):
        rows = dot(parts_of(v_ref[c].T), table_ref[...]).reshape(8, PL, N)
        for n in range(8):
            out_ref[(n + PA - rank) % 8, :, c, :] = rows[n]


def inverse_second(spectral, table):
    return pl.pallas_call(
        inverse_kernel,
        grid=(HI // 8,),
        in_specs=[
            pl.BlockSpec((GX, N, 8 * PL), lambda s: (0, 0, s)),
            pl.BlockSpec((3 * N, N), lambda s: (0, 0)),
        ],
        out_specs=pl.BlockSpec((8, PL, GX, N), lambda s: (s, 0, 0, 0)),
        out_shape=jax.ShapeDtypeStruct((HI, PL, GX, N), jnp.float32),
        compiler_params=pltpu.CompilerParams(vmem_limit_bytes=32 << 20),
        cost_estimate=pl.CostEstimate(flops=6 * 4096 * N * N, bytes_accessed=9 << 20, transcendentals=0),
        name="inverse_second",
    )(spectral, table)


def deal(pieces, block_ids):
    pieces = [pieces[-d % 8] for d in range(8)]
    for step in (1, 2, 4):
        taken = (block_ids & step) != 0
        pieces = [jnp.where(taken, pieces[(d - step) % 8], pieces[d]) for d in range(8)]
    return pieces


def choose_kernel(phase_ref, out_ref):
    slot = lax.broadcasted_iota(jnp.int32, (1, SLOTS, N), 1)
    upper = (slot == 0) & (lax.axis_index("pa") >= PA // 2)
    for c in range(GX):
        out_ref[c, 0, :ROWS] = jnp.where(upper, phase_ref[:, c, SLOTS:, :], phase_ref[:, c, :SLOTS, :])
        first = phase_ref[:, c, 0, :N // 2]
        out_ref[c, 0, ROWS] = jnp.concatenate([first[:8], first[8:]], axis=1)


def choose_phases(turned):
    shape = (GX, HI // ROWS, ROWS + 1, SLOTS, N)
    return pl.pallas_call(
        choose_kernel,
        grid=(HI // ROWS,),
        in_specs=[pl.BlockSpec((ROWS, GX, PL, N), lambda s: (s, 0, 0, 0))],
        out_specs=pl.BlockSpec((GX, 1) + shape[2:], lambda s: (0, s, 0, 0, 0)),
        out_shape=jax.ShapeDtypeStruct(shape, jnp.float32),
        compiler_params=pltpu.CompilerParams(vmem_limit_bytes=60 << 20),
        cost_estimate=pl.CostEstimate(flops=0, bytes_accessed=7 << 20, transcendentals=0),
        name="choose_phases",
    )(turned)


def turn_kernel(phase_ref, order_ref, cos_ref, sin_ref, cos0_ref, sin0_ref, lowest_ref):
    for j in range(GX):
        for s in range(HI // ROWS):
            start = j * HI + s * ROWS
            at = pl.ds(start, ROWS)
            angles = phase_ref[j, s, :ROWS].reshape(ROWS * SLOTS, N)
            high = angles.astype(jnp.bfloat16)
            rest = angles - high.astype(jnp.float32)
            mid = rest.astype(jnp.bfloat16)
            low = (rest - mid.astype(jnp.float32)).astype(jnp.bfloat16)
            angles = dot(jnp.concatenate([high, mid, low], axis=1), order_ref[...])
            cos_ref[at] = jnp.cos(angles).reshape(ROWS, SLOTS, N)
            sin_ref[at] = jnp.sin(angles).reshape(ROWS, SLOTS, N)
            first = phase_ref[j, s, :ROWS, 0, :N // 2]
            cos0_ref[at, :] = jnp.cos(first)
            sin0_ref[at, :] = jnp.sin(first)
            tail = phase_ref[j, s, ROWS]
            for n, turn in enumerate((jnp.cos(tail), jnp.sin(tail))):
                lowest_ref[n, pl.ds(start, 8), :] = turn[:, :N // 2]
                lowest_ref[n, pl.ds(start + 8, 8), :] = turn[:, N // 2:]


def turn_factors(phases, order):
    whole = pl.BlockSpec(memory_space=pltpu.VMEM)
    full = jax.ShapeDtypeStruct((N, SLOTS, N), jnp.float32)
    first = jax.ShapeDtypeStruct((N, N // 2), jnp.float32)
    return pl.pallas_call(
        turn_kernel,
        in_specs=[whole] * 2,
        out_specs=[whole] * 5,
        out_shape=[full, full, first, first, jax.ShapeDtypeStruct((2, N, N // 2), jnp.float32)],
        compiler_params=pltpu.CompilerParams(vmem_limit_bytes=24 << 20),
        cost_estimate=pl.CostEstimate(flops=0, bytes_accessed=8 << 20, transcendentals=2 * N * N * SLOTS),
        name="turn_factors",
    )(phases, order)


def middle_kernel(r_hbm, cos_hbm, sin_hbm, cos0_hbm, sin0_hbm, lowest_hbm, tables_hbm, shift_ref, fraction_ref,
                  y_hbm, buf, xa, xb, xc, cos_ref, sin_ref, cos0_ref, sin0_ref, turn1_ref, tables_ref,
                  bits_ref, w_ref, s_ref, block_sems, sems):
    half = N // 2
    special = lax.axis_index("pa") == 0
    inbound = [pltpu.make_async_copy(r_hbm.at[a], buf.at[a], block_sems.at[a]) for a in range(GX)]
    tiles = N // KTILE
    transfers = [
        (tables_hbm, tables_ref), (cos_hbm, cos_ref), (sin_hbm, sin_ref),
        (cos0_hbm, cos0_ref), (sin0_hbm, sin0_ref), (lowest_hbm, turn1_ref),
    ]
    extras = [pltpu.make_async_copy(source, target, sems.at[n]) for n, (source, target) in enumerate(transfers)]
    for copy in inbound + extras:
        copy.start()
    fe_ref, fo_ref, ie_ref, io_ref, fr_ref, ir_ref = (tables_ref.at[n] for n in range(6))

    steps = jnp.broadcast_to(shift_ref[...], (8, N)) + SMAX
    for bit in range(5):
        bits_ref[bit] = (steps >> bit) & 1
    for k, weight in enumerate(cubic_weights(jnp.broadcast_to(fraction_ref[...], (8, N)))):
        w_ref[k] = weight
    block_ids = lax.broadcasted_iota(jnp.int32, (8, 128), 1) // PL

    def gather(a, g, carry):
        step = a * 4 + g
        lane = pl.multiple_of(g * 128, 128)
        row = PAD_LO + step * 8
        for mh in range(2):
            for bh in range(2):
                pieces = [buf[a, bh * 8 + j, mh * 8:mh * 8 + 8, pl.ds(lane, 128)] for j in range(8)]
                pieces = deal(pieces, block_ids)
                for j in range(8):
                    piece = pltpu.roll(pieces[j], 128 - PL * j, 1) if j else pieces[j]
                    xa[bh, row + j, mh * 8:mh * 8 + 8, :] = piece
        return carry

    def wrap(x):
        x[:, 0:PAD_LO] = x[:, N:N + PAD_LO]
        x[:, PAD_LO + N:PAD_LO + N + PAD_HI] = x[:, PAD_LO:PAD_LO + PAD_HI]

    def drift(x, first):
        need = TILE + 3
        for mh in range(2):
            for ph in range(2):
                ms = slice(mh * 8, mh * 8 + 8)
                ps = slice(ph * 128, ph * 128 + 128)
                rows = need + 31
                z = x[ph, pl.ds(first + PAD_LO + SMAX - 1 - 31, rows), ms, :]
                for bit in (4, 3, 2, 1, 0):
                    size = 1 << bit
                    taken = bits_ref[bit, :, ps] != 0
                    z = jnp.where(taken[None], z[:rows - size], z[size:])
                    rows = rows - size
                total = w_ref[0, :, ps][None] * z[0:TILE]
                for k in (1, 2, 3):
                    total = total + w_ref[k, :, ps][None] * z[k:k + TILE]
                xb[ph, pl.ds(first, TILE), ms, :] = total

    def turned(y, c, s, forward_ref, inverse_ref):
        z = three_dots(y, forward_ref)
        zr, zi = z[:, :half], z[:, half:]
        g = jnp.concatenate([zr * c - zi * s, zr * s + zi * c], axis=1)
        return three_dots(g, inverse_ref)

    def kick(to_ref, first):
        rows = KTILE * SLOTS
        at = pl.ds(first, KTILE)
        low, high = (
            jnp.concatenate([xb[h, at, m:m + 8, :].reshape(rows, half) for m in (0, 8)], axis=1)
            for h in range(2)
        )
        cos = cos_ref[at].reshape(rows, N)
        sin = sin_ref[at].reshape(rows, N)
        even = turned(low + high, cos[:, :half], sin[:, :half], fe_ref, ie_ref)
        odd = turned(low - high, cos[:, half:], sin[:, half:], fo_ref, io_ref)
        out = pl.ds(first + PAD_LO, KTILE)
        for h, both in enumerate((even + odd, even - odd)):
            to_ref[h, out, 0:8, :] = both[:, :half].reshape(KTILE, 8, half)
            to_ref[h, out, 8:16, :] = both[:, half:].reshape(KTILE, 8, half)

    def shared_slot():
        flat = xb.reshape(2 * N * M, half)
        x = jnp.concatenate([
            jnp.concatenate([flat[pl.ds(h * N * M + row, N, stride=M), :] for h in range(2)], axis=1)
            for row in (0, SLOTS)
        ], axis=0)
        c = jnp.concatenate([cos0_ref[...], turn1_ref[0]], axis=0)
        s = jnp.concatenate([sin0_ref[...], turn1_ref[1]], axis=0)
        s_ref[...] = turned(x, c, s, fr_ref, ir_ref)

    def place_shared(to_ref, first, count):
        flat = to_ref.reshape(2 * to_ref.shape[1] * M, half)
        for h in range(2):
            for part in range(2):
                start = (h * to_ref.shape[1] + PAD_LO + first) * M + part * SLOTS
                flat[pl.ds(start, count, stride=M), :] = s_ref[part * N + first:part * N + first + count,
                                                               h * half:h * half + half]

    def scatter(a, g):
        lane = g * 128
        row = PAD_LO + a * HI + g * 8
        for mh in range(2):
            for bh in range(2):
                pieces = [xa[bh, row + j, mh * 8:mh * 8 + 8, :] for j in range(8)]
                pieces = [pltpu.roll(pieces[j], PL * j, 1) if j else pieces[j] for j in range(8)]
                pieces = deal(pieces, block_ids)
                for j in range(8):
                    buf[a, bh * 8 + j, mh * 8:mh * 8 + 8, lane:lane + 128] = pieces[j]

    def drift_tile(x, tile):
        for part in range(KTILE // TILE):
            drift(x, tile * KTILE + part * TILE)

    for a in range(GX):
        inbound[a].wait()
        lax.fori_loop(0, HI // 8, functools.partial(gather, a), 0, unroll=2)
    done = (tiles - 1) * KTILE
    outbound = [pltpu.make_async_copy(buf.at[a], y_hbm.at[a], block_sems.at[a]) for a in range(GX)]
    for substep in range(STEPS):
        source, target = (xa, xc) if substep % 2 == 0 else (xc, xa)
        last = substep + 1 == STEPS
        wrap(source)
        drift_tile(source, 0)
        if substep == 0:
            for copy in extras:
                copy.wait()
        for tile in range(tiles - 1):
            drift_tile(source, tile + 1)
            if tile == tiles - 2:
                shared_slot()
            kick(target, tile * KTILE)

        if last:
            @pl.when(special)
            def _():
                place_shared(target, 0, done)

        kick(target, done)
        if last:
            for a in range(done // HI):
                for g in range(HI // 8):
                    scatter(a, g)
                outbound[a].start()

        @pl.when(special)
        def _():
            if last:
                place_shared(target, done, KTILE)
            else:
                place_shared(target, 0, N)

    for a in range(done // HI, GX):
        for g in range(HI // 8):
            scatter(a, g)
        outbound[a].start()
    for copy in outbound:
        copy.wait()


def middle(received, factors, lowest, tables, shifts, fractions):
    anywhere = pl.BlockSpec(memory_space=pl.ANY)
    whole = pl.BlockSpec(memory_space=pltpu.VMEM)
    return pl.pallas_call(
        middle_kernel,
        in_specs=[anywhere] * 7 + [whole] * 2,
        out_specs=anywhere,
        out_shape=jax.ShapeDtypeStruct((GX, PA, M, LANES), jnp.float32),
        scratch_shapes=[
            pltpu.VMEM((GX, PA, M, LANES), jnp.float32),
            pltpu.VMEM((2, PAD_LO + N + PAD_HI, M, N // 2), jnp.float32),
            pltpu.VMEM((2, N, M, N // 2), jnp.float32),
            pltpu.VMEM((2, PAD_LO + N + PAD_HI, M, N // 2), jnp.float32),
            pltpu.VMEM((N, SLOTS, N), jnp.float32),
            pltpu.VMEM((N, SLOTS, N), jnp.float32),
        ] + [pltpu.VMEM((N, N // 2), jnp.float32)] * 2 + [
            pltpu.VMEM((2, N, N // 2), jnp.float32),
            pltpu.VMEM((6, 2 * N, N), jnp.bfloat16),
            pltpu.VMEM((5, 8, N), jnp.int32),
            pltpu.VMEM((4, 8, N), jnp.float32),
            pltpu.VMEM((2 * N, N), jnp.float32),
            pltpu.SemaphoreType.DMA((GX,)),
            pltpu.SemaphoreType.DMA((6,)),
        ],
        compiler_params=pltpu.CompilerParams(vmem_limit_bytes=60 << 20),
        cost_estimate=pl.CostEstimate(flops=24 * 2048 * 2 * N * N, bytes_accessed=14 << 20, transcendentals=0),
        name="middle",
    )(received, *factors, lowest, tables, shifts, fractions)


def cubic_weights(fraction):
    return (
        -fraction * (fraction - 1.0) * (fraction - 2.0) / 6.0,
        (fraction + 1.0) * (fraction - 1.0) * (fraction - 2.0) / 2.0,
        -(fraction + 1.0) * fraction * (fraction - 2.0) / 2.0,
        (fraction + 1.0) * fraction * (fraction - 1.0) / 6.0,
    )


def shards(density, shifts, fractions, kick_phase):
    forward, inverse = (jnp.asarray(t) for t in second_tables())
    (fe, ie), (fo, io), (fr, ir) = paired(True), paired(False), real_tables()
    tables = jnp.asarray(np.stack([fe, fo, ie, io, fr, ir]))
    chosen = choose_phases(kick_phase.transpose(0, 2, 3, 1))
    chosen, density = lax.optimization_barrier((chosen, density))
    phases = lax.all_to_all(chosen, "gx", 0, 0, tiled=True)
    spectral = forward_second(density, forward).reshape(GX * PA, M, LANES)
    phases, spectral = lax.optimization_barrier((phases, spectral))
    received = lax.all_to_all(spectral, ("gx", "pa"), 0, 0, tiled=True)
    received = received.reshape(GX, PA, M, LANES)
    *factors, lowest = turn_factors(phases, jnp.asarray(parity_order()))
    lowest = lax.ppermute(lowest, "pa", [(PA // 2, 0)])
    sent = middle(received, factors, lowest, tables, shifts.reshape(1, N), fractions.reshape(1, N))
    sent = sent.reshape(GX * PA, M, LANES)
    returned = lax.all_to_all(sent, ("gx", "pa"), 0, 0, tiled=True)
    return inverse_second(returned.reshape(GX, N, LANES), inverse)


def solution(mesh):
    placed = (P("gx", "pa", None, None), P(), P(), P("gx", None, None, "pa"))
    return jax.shard_map(
        shards, mesh=mesh, in_specs=placed, out_specs=P("gx", "pa", None, None), check_vma=False
    )
```

```python
import functools
import math

import jax
import jax.numpy as jnp
import ml_dtypes
import numpy as np
from jax import lax
from jax.experimental import pallas as pl
from jax.experimental.pallas import tpu as pltpu
from jax.sharding import PartitionSpec as P

STEPS = 2
N = 256
GX = 8
PA = 16
HI = N // GX
PL = N // PA
SLOTS = 8
M = 2 * SLOTS
LANES = HI * PL
PAD_LO = 24
PAD_HI = 16
SMAX = 10
TILE = 32
KTILE = 64
ROWS = 16


def split_table(table):
    high = table.astype(ml_dtypes.bfloat16)
    low = (table - high.astype(np.float64)).astype(ml_dtypes.bfloat16)
    return high, low


def stacked(table):
    high, low = split_table(table)
    return np.concatenate([high, high, low], axis=0)


def both_parts(table):
    return np.concatenate(split_table(table), axis=0)


def owned_columns(device):
    start = PL * device + (0 if device < PA // 2 else 1)
    return [start + slot for slot in range(SLOTS)]


def second_tables():
    q = np.arange(N)
    forward = np.zeros((N, N))
    inverse = np.zeros((N, N))
    scale = 1.0 / N ** (STEPS + 1)
    for device in range(PA):
        for slot, col in enumerate(owned_columns(device)):
            angle = 2.0 * math.pi * (q * col % N) / N
            re_row = device * M + slot
            im_row = re_row + SLOTS
            if col == 0:
                half = 1.0 - 2.0 * (q % 2)
                forward[:, re_row] = 1.0
                forward[:, im_row] = half
                inverse[re_row] = scale
                inverse[im_row] = scale * half
            else:
                forward[:, re_row] = np.cos(angle)
                forward[:, im_row] = -np.sin(angle)
                inverse[re_row] = 2.0 * scale * np.cos(angle)
                inverse[im_row] = -2.0 * scale * np.sin(angle)
    return stacked(forward), stacked(inverse)


def paired(even):
    half = np.arange(N // 2)
    k = 2 * half + (0 if even else 1)
    angle = 2.0 * math.pi * (half[:, None] * k[None, :] % N) / N
    cos, sin = np.cos(angle), np.sin(angle)
    forward = np.block([[cos, -sin], [sin, cos]])
    inverse = np.block([[cos.T, sin.T], [-sin.T, cos.T]])
    return both_parts(forward), both_parts(inverse)


def real_tables():
    p = np.arange(N)
    k = np.arange(N // 2)
    angle = 2.0 * math.pi * (p[:, None] * k[None, :] % N) / N
    last = (1.0 - 2.0 * (p % 2))[:, None]
    cos, sin = np.cos(angle), np.sin(angle)
    forward = np.concatenate([cos, last, -sin[:, 1:]], axis=1)
    inverse = np.concatenate([cos[:, :1], 2.0 * cos[:, 1:], last, -2.0 * sin[:, 1:]], axis=1).T
    return both_parts(forward), both_parts(inverse)


def parity_order():
    table = np.zeros((N, N))
    k = np.concatenate([np.arange(0, N, 2), np.arange(1, N, 2)])
    table[k, np.arange(N)] = 1.0
    return np.concatenate([table] * 3, axis=0).astype(ml_dtypes.bfloat16)


def parts_of(values):
    high = values.astype(jnp.bfloat16)
    low = (values - high.astype(jnp.float32)).astype(jnp.bfloat16)
    return jnp.concatenate([high, low, high], axis=1)


def dot(a, b):
    return jnp.dot(a, b, preferred_element_type=jnp.float32)


def three_dots(values, table_ref):
    high = values.astype(jnp.bfloat16)
    low = (values - high.astype(jnp.float32)).astype(jnp.bfloat16)
    top = table_ref[:N]
    return dot(high, top) + dot(low, top) + dot(high, table_ref[N:])


def forward_kernel(low_ref, high_ref, table_ref, out_ref):
    low = low_ref.reshape(8 * PL * GX, N // 2)
    high = high_ref.reshape(8 * PL * GX, N // 2)
    rank = lax.axis_index("pa")
    for c in range(GX):
        rows = []
        for n in range(8):
            at = pl.ds((n + PA - rank) % 8 * (PL * GX) + c, PL, stride=GX)
            rows.append(jnp.concatenate([low[at, :], high[at, :]], axis=1))
        rows = jnp.concatenate(rows, axis=0)
        out_ref[c] = dot(parts_of(rows), table_ref[...]).T


def forward_second(density, table):
    return pl.pallas_call(
        forward_kernel,
        grid=(HI // 8,),
        in_specs=[
            pl.BlockSpec((8, PL, GX, N // 2), lambda s: (s, 0, 0, 0)),
            pl.BlockSpec((8, PL, GX, N // 2), lambda s: (s, 0, 0, 1)),
            pl.BlockSpec((3 * N, N), lambda s: (0, 0)),
        ],
        out_specs=pl.BlockSpec((GX, N, 8 * PL), lambda s: (0, 0, s)),
        out_shape=jax.ShapeDtypeStruct((GX, N, LANES), jnp.float32),
        compiler_params=pltpu.CompilerParams(vmem_limit_bytes=60 << 20),
        cost_estimate=pl.CostEstimate(flops=6 * 4096 * N * N, bytes_accessed=9 << 20, transcendentals=0),
        name="forward_second",
    )(density, density, table)


def inverse_kernel(v_ref, table_ref, out_ref):
    rank = lax.axis_index("pa")
    for c in range(GX):
        rows = dot(parts_of(v_ref[c].T), table_ref[...]).reshape(8, PL, N)
        for n in range(8):
            out_ref[(n + PA - rank) % 8, :, c, :] = rows[n]


def inverse_second(spectral, table):
    return pl.pallas_call(
        inverse_kernel,
        grid=(HI // 8,),
        in_specs=[
            pl.BlockSpec((GX, N, 8 * PL), lambda s: (0, 0, s)),
            pl.BlockSpec((3 * N, N), lambda s: (0, 0)),
        ],
        out_specs=pl.BlockSpec((8, PL, GX, N), lambda s: (s, 0, 0, 0)),
        out_shape=jax.ShapeDtypeStruct((HI, PL, GX, N), jnp.float32),
        compiler_params=pltpu.CompilerParams(vmem_limit_bytes=32 << 20),
        cost_estimate=pl.CostEstimate(flops=6 * 4096 * N * N, bytes_accessed=9 << 20, transcendentals=0),
        name="inverse_second",
    )(spectral, table)


def deal(pieces, block_ids):
    pieces = [pieces[-d % 8] for d in range(8)]
    for step in (1, 2, 4):
        taken = (block_ids & step) != 0
        pieces = [jnp.where(taken, pieces[(d - step) % 8], pieces[d]) for d in range(8)]
    return pieces


def choose_kernel(phase_ref, out_ref):
    low = lax.axis_index("pa") < PA // 2
    for c in range(GX):
        out_ref[c, 0, :ROWS] = jnp.where(low, phase_ref[:, c, 0:SLOTS, :], phase_ref[:, c, 1:SLOTS + 1, :])
        first = phase_ref[:, c, 0, :N // 2]
        out_ref[c, 0, ROWS] = jnp.concatenate([first[:8], first[8:]], axis=1)


def choose_phases(turned):
    shape = (GX, HI // ROWS, ROWS + 1, SLOTS, N)
    return pl.pallas_call(
        choose_kernel,
        grid=(HI // ROWS,),
        in_specs=[pl.BlockSpec((ROWS, GX, PL, N), lambda s: (s, 0, 0, 0))],
        out_specs=pl.BlockSpec((GX, 1) + shape[2:], lambda s: (0, s, 0, 0, 0)),
        out_shape=jax.ShapeDtypeStruct(shape, jnp.float32),
        compiler_params=pltpu.CompilerParams(vmem_limit_bytes=60 << 20),
        cost_estimate=pl.CostEstimate(flops=0, bytes_accessed=7 << 20, transcendentals=0),
        name="choose_phases",
    )(turned)


def turn_kernel(phase_ref, order_ref, cos_ref, sin_ref, cos0_ref, sin0_ref, lowest_ref):
    for j in range(GX):
        for s in range(HI // ROWS):
            start = j * HI + s * ROWS
            at = pl.ds(start, ROWS)
            angles = phase_ref[j, s, :ROWS].reshape(ROWS * SLOTS, N)
            high = angles.astype(jnp.bfloat16)
            rest = angles - high.astype(jnp.float32)
            mid = rest.astype(jnp.bfloat16)
            low = (rest - mid.astype(jnp.float32)).astype(jnp.bfloat16)
            angles = dot(jnp.concatenate([high, mid, low], axis=1), order_ref[...])
            cos_ref[at] = jnp.cos(angles).reshape(ROWS, SLOTS, N)
            sin_ref[at] = jnp.sin(angles).reshape(ROWS, SLOTS, N)
            first = phase_ref[j, s, :ROWS, 0, :N // 2]
            cos0_ref[at, :] = jnp.cos(first)
            sin0_ref[at, :] = jnp.sin(first)
            tail = phase_ref[j, s, ROWS]
            for n, turn in enumerate((jnp.cos(tail), jnp.sin(tail))):
                lowest_ref[n, pl.ds(start, 8), :] = turn[:, :N // 2]
                lowest_ref[n, pl.ds(start + 8, 8), :] = turn[:, N // 2:]


def turn_factors(phases, order):
    whole = pl.BlockSpec(memory_space=pltpu.VMEM)
    full = jax.ShapeDtypeStruct((N, SLOTS, N), jnp.float32)
    first = jax.ShapeDtypeStruct((N, N // 2), jnp.float32)
    return pl.pallas_call(
        turn_kernel,
        in_specs=[whole] * 2,
        out_specs=[whole] * 5,
        out_shape=[full, full, first, first, jax.ShapeDtypeStruct((2, N, N // 2), jnp.float32)],
        compiler_params=pltpu.CompilerParams(vmem_limit_bytes=24 << 20),
        cost_estimate=pl.CostEstimate(flops=0, bytes_accessed=8 << 20, transcendentals=2 * N * N * SLOTS),
        name="turn_factors",
    )(phases, order)


def middle_kernel(r_hbm, cos_hbm, sin_hbm, cos0_hbm, sin0_hbm, lowest_hbm, tables_hbm, shift_ref, fraction_ref,
                  y_hbm, buf, xa, xb, xc, cos_ref, sin_ref, cos0_ref, sin0_ref, turn1_ref, tables_ref,
                  bits_ref, w_ref, s_ref, block_sems, sems):
    half = N // 2
    special = lax.axis_index("pa") == 0
    inbound = [pltpu.make_async_copy(r_hbm.at[a], buf.at[a], block_sems.at[a]) for a in range(GX)]
    tiles = N // KTILE
    transfers = [
        (tables_hbm, tables_ref), (cos_hbm, cos_ref), (sin_hbm, sin_ref),
        (cos0_hbm, cos0_ref), (sin0_hbm, sin0_ref), (lowest_hbm, turn1_ref),
    ]
    extras = [pltpu.make_async_copy(source, target, sems.at[n]) for n, (source, target) in enumerate(transfers)]
    for copy in inbound + extras:
        copy.start()
    fe_ref, fo_ref, ie_ref, io_ref, fr_ref, ir_ref = (tables_ref.at[n] for n in range(6))

    steps = jnp.broadcast_to(shift_ref[...], (8, N)) + SMAX
    for bit in range(5):
        bits_ref[bit] = (steps >> bit) & 1
    for k, weight in enumerate(cubic_weights(jnp.broadcast_to(fraction_ref[...], (8, N)))):
        w_ref[k] = weight
    block_ids = lax.broadcasted_iota(jnp.int32, (8, 128), 1) // PL

    def gather(a, g, carry):
        step = a * 4 + g
        lane = pl.multiple_of(g * 128, 128)
        row = PAD_LO + step * 8
        for mh in range(2):
            for bh in range(2):
                pieces = [buf[a, bh * 8 + j, mh * 8:mh * 8 + 8, pl.ds(lane, 128)] for j in range(8)]
                pieces = deal(pieces, block_ids)
                for j in range(8):
                    piece = pltpu.roll(pieces[j], 128 - PL * j, 1) if j else pieces[j]
                    xa[bh, row + j, mh * 8:mh * 8 + 8, :] = piece
        return carry

    def wrap(x):
        x[:, 0:PAD_LO] = x[:, N:N + PAD_LO]
        x[:, PAD_LO + N:PAD_LO + N + PAD_HI] = x[:, PAD_LO:PAD_LO + PAD_HI]

    def drift(x, first):
        need = TILE + 3
        for mh in range(2):
            for ph in range(2):
                ms = slice(mh * 8, mh * 8 + 8)
                ps = slice(ph * 128, ph * 128 + 128)
                rows = need + 31
                z = x[ph, pl.ds(first + PAD_LO + SMAX - 1 - 31, rows), ms, :]
                for bit in (4, 3, 2, 1, 0):
                    size = 1 << bit
                    taken = bits_ref[bit, :, ps] != 0
                    z = jnp.where(taken[None], z[:rows - size], z[size:])
                    rows = rows - size
                total = w_ref[0, :, ps][None] * z[0:TILE]
                for k in (1, 2, 3):
                    total = total + w_ref[k, :, ps][None] * z[k:k + TILE]
                xb[ph, pl.ds(first, TILE), ms, :] = total

    def turned(y, c, s, forward_ref, inverse_ref):
        z = three_dots(y, forward_ref)
        zr, zi = z[:, :half], z[:, half:]
        g = jnp.concatenate([zr * c - zi * s, zr * s + zi * c], axis=1)
        return three_dots(g, inverse_ref)

    def kick(to_ref, first):
        rows = KTILE * SLOTS
        at = pl.ds(first, KTILE)
        low, high = (
            jnp.concatenate([xb[h, at, m:m + 8, :].reshape(rows, half) for m in (0, 8)], axis=1)
            for h in range(2)
        )
        cos = cos_ref[at].reshape(rows, N)
        sin = sin_ref[at].reshape(rows, N)
        even = turned(low + high, cos[:, :half], sin[:, :half], fe_ref, ie_ref)
        odd = turned(low - high, cos[:, half:], sin[:, half:], fo_ref, io_ref)
        out = pl.ds(first + PAD_LO, KTILE)
        for h, both in enumerate((even + odd, even - odd)):
            to_ref[h, out, 0:8, :] = both[:, :half].reshape(KTILE, 8, half)
            to_ref[h, out, 8:16, :] = both[:, half:].reshape(KTILE, 8, half)

    def shared_slot():
        flat = xb.reshape(2 * N * M, half)
        x = jnp.concatenate([
            jnp.concatenate([flat[pl.ds(h * N * M + row, N, stride=M), :] for h in range(2)], axis=1)
            for row in (0, SLOTS)
        ], axis=0)
        c = jnp.concatenate([cos0_ref[...], turn1_ref[0]], axis=0)
        s = jnp.concatenate([sin0_ref[...], turn1_ref[1]], axis=0)
        s_ref[...] = turned(x, c, s, fr_ref, ir_ref)

    def place_shared(to_ref, first, count):
        flat = to_ref.reshape(2 * to_ref.shape[1] * M, half)
        for h in range(2):
            for part in range(2):
                start = (h * to_ref.shape[1] + PAD_LO + first) * M + part * SLOTS
                flat[pl.ds(start, count, stride=M), :] = s_ref[part * N + first:part * N + first + count,
                                                               h * half:h * half + half]

    def scatter(a, g):
        lane = g * 128
        row = PAD_LO + a * HI + g * 8
        for mh in range(2):
            for bh in range(2):
                pieces = [xa[bh, row + j, mh * 8:mh * 8 + 8, :] for j in range(8)]
                pieces = [pltpu.roll(pieces[j], PL * j, 1) if j else pieces[j] for j in range(8)]
                pieces = deal(pieces, block_ids)
                for j in range(8):
                    buf[a, bh * 8 + j, mh * 8:mh * 8 + 8, lane:lane + 128] = pieces[j]

    def drift_tile(x, tile):
        for part in range(KTILE // TILE):
            drift(x, tile * KTILE + part * TILE)

    for a in range(GX):
        inbound[a].wait()
        lax.fori_loop(0, HI // 8, functools.partial(gather, a), 0, unroll=2)
    done = (tiles - 1) * KTILE
    outbound = [pltpu.make_async_copy(buf.at[a], y_hbm.at[a], block_sems.at[a]) for a in range(GX)]
    for substep in range(STEPS):
        source, target = (xa, xc) if substep % 2 == 0 else (xc, xa)
        last = substep + 1 == STEPS
        wrap(source)
        drift_tile(source, 0)
        if substep == 0:
            for copy in extras:
                copy.wait()
        for tile in range(tiles - 1):
            if tile == tiles - 2:
                drift_tile(source, tile + 1)
                shared_slot()
            kick(target, tile * KTILE)
            if tile != tiles - 2:
                drift_tile(source, tile + 1)

        if last:
            @pl.when(special)
            def _():
                place_shared(target, 0, done)

        kick(target, done)
        if last:
            for a in range(done // HI):
                for g in range(HI // 8):
                    scatter(a, g)
                outbound[a].start()

        @pl.when(special)
        def _():
            if last:
                place_shared(target, done, KTILE)
            else:
                place_shared(target, 0, N)

    for a in range(done // HI, GX):
        for g in range(HI // 8):
            scatter(a, g)
        outbound[a].start()
    for copy in outbound:
        copy.wait()


def middle(received, factors, lowest, tables, shifts, fractions):
    anywhere = pl.BlockSpec(memory_space=pl.ANY)
    whole = pl.BlockSpec(memory_space=pltpu.VMEM)
    return pl.pallas_call(
        middle_kernel,
        in_specs=[anywhere] * 7 + [whole] * 2,
        out_specs=anywhere,
        out_shape=jax.ShapeDtypeStruct((GX, PA, M, LANES), jnp.float32),
        scratch_shapes=[
            pltpu.VMEM((GX, PA, M, LANES), jnp.float32),
            pltpu.VMEM((2, PAD_LO + N + PAD_HI, M, N // 2), jnp.float32),
            pltpu.VMEM((2, N, M, N // 2), jnp.float32),
            pltpu.VMEM((2, PAD_LO + N + PAD_HI, M, N // 2), jnp.float32),
            pltpu.VMEM((N, SLOTS, N), jnp.float32),
            pltpu.VMEM((N, SLOTS, N), jnp.float32),
        ] + [pltpu.VMEM((N, N // 2), jnp.float32)] * 2 + [
            pltpu.VMEM((2, N, N // 2), jnp.float32),
            pltpu.VMEM((6, 2 * N, N), jnp.bfloat16),
            pltpu.VMEM((5, 8, N), jnp.int32),
            pltpu.VMEM((4, 8, N), jnp.float32),
            pltpu.VMEM((2 * N, N), jnp.float32),
            pltpu.SemaphoreType.DMA((GX,)),
            pltpu.SemaphoreType.DMA((6,)),
        ],
        compiler_params=pltpu.CompilerParams(vmem_limit_bytes=60 << 20),
        cost_estimate=pl.CostEstimate(flops=24 * 2048 * 2 * N * N, bytes_accessed=14 << 20, transcendentals=0),
        name="middle",
    )(received, *factors, lowest, tables, shifts, fractions)


def cubic_weights(fraction):
    return (
        -fraction * (fraction - 1.0) * (fraction - 2.0) / 6.0,
        (fraction + 1.0) * (fraction - 1.0) * (fraction - 2.0) / 2.0,
        -(fraction + 1.0) * fraction * (fraction - 2.0) / 2.0,
        (fraction + 1.0) * fraction * (fraction - 1.0) / 6.0,
    )


def shards(density, shifts, fractions, kick_phase):
    forward, inverse = (jnp.asarray(t) for t in second_tables())
    (fe, ie), (fo, io), (fr, ir) = paired(True), paired(False), real_tables()
    tables = jnp.asarray(np.stack([fe, fo, ie, io, fr, ir]))
    chosen = choose_phases(kick_phase.transpose(0, 2, 3, 1))
    chosen, density = lax.optimization_barrier((chosen, density))
    phases = lax.all_to_all(chosen, "gx", 0, 0, tiled=True)
    spectral = forward_second(density, forward).reshape(GX * PA, M, LANES)
    phases, spectral = lax.optimization_barrier((phases, spectral))
    received = lax.all_to_all(spectral, ("gx", "pa"), 0, 0, tiled=True)
    received = received.reshape(GX, PA, M, LANES)
    *factors, lowest = turn_factors(phases, jnp.asarray(parity_order()))
    lowest = lax.ppermute(lowest, "pa", [(PA // 2, 0)])
    sent = middle(received, factors, lowest, tables, shifts.reshape(1, N), fractions.reshape(1, N))
    sent = sent.reshape(GX * PA, M, LANES)
    returned = lax.all_to_all(sent, ("gx", "pa"), 0, 0, tiled=True)
    return inverse_second(returned.reshape(GX, N, LANES), inverse)


def solution(mesh):
    placed = (P("gx", "pa", None, None), P(), P(), P("gx", None, None, "pa"))
    return jax.shard_map(
        shards, mesh=mesh, in_specs=placed, out_specs=P("gx", "pa", None, None), check_vma=False
    )
```
